1024 devices in a mesh: lat: 64 (over z, y), lon: 16 (over x, core).
Axes of the slice: x: 8, y: 8, z: 8, core: 2. Of those that a mesh axis runs over, the one named last changes fastest.
Arguments:
- spec: float32 [4, 2, 640, 1344], P(None, None, 'lat', 'lon'), may hold values from -6 to 6
- legendre: bfloat16 [640, 1344, 1280], P('lat', 'lon'), may hold values from -0.25 to 0.25
- wave_pairs: int32 [640], replicated, may hold values from 0 to 639, each once
- row_waves: int32 [2560], P('lat'), may hold values from 16 to 1280, as said below
- forcing: float32 [4, 2560, 5120], P(None, 'lat', 'lon'), may hold values from -6 to 6
- helm_coef: float32 [4], replicated, may hold values from 6.1035155e-07 to 4.8828124e-06
Outputs:
- grid_field: float32 [4, 2560, 5120], P(None, 'lat', 'lon')
- spec_new: float32 [4, 2, 640, 1344], P(None, None, 'lat', 'lon')
The draws below stay inside these ranges and needn't reach their ends.
Inputs may be any that keep to these rules, and one draw needn't show every extreme that they name: Each value appears once; row s holds the wavenumbers wave_pairs[s] and 1279 - wave_pairs[s]. `row_waves`: rows near the equator resolve all 1280 wavenumbers.
All inputs are finite; a program needn't handle non-finite values.
Results may differ from the reference program's by a relative error of at most 0.028.
Values may be sent and summed in bfloat16 or wider, within the bound.
A program may use at most 64 MiB of HBM per device.

```python
import math
import jax
import jax.numpy as jnp
from jax import lax

M = 1280
NLAT = 2560
NLON = 5120
F = 4
PAIRS = 640
NPAD = 1344
N_LON = 16


def draw_row_waves(key, part):
    row_index = jnp.arange(NLAT, dtype=jnp.int32)
    pole_gap = jnp.minimum(row_index, NLAT - 1 - row_index)
    jitter = jax.random.randint(key, (NLAT,), 0, M // 4, dtype=jnp.int32)
    jitter = jnp.where(pole_gap == 0, 0, jitter)
    return jnp.minimum(M, 16 + 2 * pole_gap * M // NLAT + jitter).astype(jnp.int32)


def levels(own_key, extent, split, smallest, high):
    level, own = 1.0, jax.random.fold_in(own_key, 6)
    for dim, parts in split:
        draws = jnp.exp(jax.random.uniform(jax.random.fold_in(own, dim), (parts,), jnp.float32, smallest / len(split), high / len(split)))
        level = level * jnp.repeat(draws, extent[dim] // parts).reshape([-1 if axis == dim else 1 for axis in range(len(extent))])
    return level


def centred(key, extent, deviation, most, shards=(), held_as=jnp.bfloat16):
    drawn = deviation * jax.random.normal(key, extent, jnp.float32)
    if shards:
        drawn = drawn * levels(key, extent, shards, -0.22, 0.18)
    return jnp.clip(drawn, -most, most).astype(held_as)


def setup_inputs(seed: int = 0) -> dict:
    keys = jax.random.split(jax.random.key(seed), 7)
    return {
        "spec": centred(keys[0], (F, 2, PAIRS, NPAD), 1.0, 6.0, ((2, 64), (3, 16)), jnp.float32),
        "legendre": centred(keys[1], (PAIRS, NPAD, NLAT // 2), (M // 2) ** -0.5, 0.25, ((0, 64), (1, 16))),
        "wave_pairs": jax.random.permutation(keys[2], PAIRS).astype(jnp.int32),
        "row_waves": draw_row_waves(jax.random.fold_in(keys[6], 71), 0),
        "forcing": centred(keys[4], (F, NLAT, NLON), 1.0, 6.0, ((1, 64), (2, 16)), jnp.float32),
        "helm_coef": jnp.clip(jnp.exp(jax.random.uniform(keys[5], (F,), jnp.float32, math.log(6.103515488575795e-07), math.log(4.882812390860636e-06))), 6.103515488575795e-07, 4.882812390860636e-06),
    }


def column_info(pair_values, columns):
    boundary = M - pair_values[:, None]
    first_part = columns[None, :] < boundary
    valid_cols = columns[None, :] < M + 1
    second_part = jnp.logical_and(valid_cols, jnp.logical_not(first_part))
    offset = jnp.where(first_part, columns[None, :], columns[None, :] - boundary)
    parity = (1 - 2 * (offset % 2)).astype(jnp.float32)
    degree = jnp.where(first_part, pair_values[:, None] + columns[None, :], columns[None, :] - 1)
    return (first_part.astype(jnp.float32), second_part.astype(jnp.float32), parity, degree.astype(jnp.float32))

def wave_numbers(pair_values):
    return jnp.stack([pair_values, M - 1 - pair_values], axis=-1)

def angles(wave_table, positions, length):
    winding = wave_table[..., None] * positions % length
    return winding.astype(jnp.float32) * (2.0 * math.pi / length)

def reference(spec, legendre, wave_pairs, row_waves, forcing, helm_coef):
    columns = jnp.arange(NPAD, dtype=jnp.int32)
    first_part, second_part, parity, degree = column_info(wave_pairs, columns)
    up_scale = 0.5 / math.sqrt(M)
    half_lats = NLAT // 2
    col_width = NPAD // N_LON
    coefficients = jnp.transpose(spec.astype(jnp.bfloat16), (2, 0, 1, 3))

    def inverse_slot(inputs):
        basis, values, part_one, part_two, signs = inputs
        selector = jnp.stack([part_one, part_two])
        flip_signs = jnp.stack([jnp.ones_like(signs), signs])
        factor = selector[:, None, :] * flip_signs[None, :, :]
        mixed_terms = factor[:, :, None, None, :] * values.astype(jnp.float32)[None, None]
        mixed_terms = mixed_terms.reshape(2, 2, F, 2, N_LON, col_width)
        blocks = basis.astype(jnp.float32).reshape(N_LON, col_width, half_lats)
        term_sums = jnp.einsum('qhfrgc,gck->gqhfrk', mixed_terms, blocks) * up_scale
        term_sums = lax.optimization_barrier(term_sums.astype(jnp.bfloat16)).astype(jnp.float32)
        return lax.optimization_barrier(jnp.sum(term_sums, axis=0))
    slot_sums = lax.map(inverse_slot, (legendre, coefficients, first_part, second_part, parity))
    north_half = slot_sums[:, :, 0]
    south_half = jnp.flip(slot_sums[:, :, 1], axis=-1)
    fourier = jnp.concatenate([north_half, south_half], axis=-1)
    wave_table = wave_numbers(wave_pairs)
    kept_mask = (wave_table[:, :, None] < row_waves[None, None, :]).astype(jnp.float32)
    fourier = (fourier * kept_mask[:, :, None, None, :]).astype(jnp.bfloat16)
    positions = jnp.arange(NLON, dtype=jnp.int32)
    phases = angles(wave_table, positions, NLON)
    weight = jnp.where(wave_table == 0, 1.0, 2.0).astype(jnp.float32)[..., None]
    forward_table = jnp.stack([weight * jnp.cos(phases), -weight * jnp.sin(phases)]).astype(jnp.bfloat16)
    grid_field = jnp.einsum('pqfrl,rpqx->flx', fourier.astype(jnp.float32), forward_table.astype(jnp.float32))
    tendency = (forcing - 0.5 * grid_field * grid_field).astype(jnp.bfloat16)
    back_table = (jnp.stack([jnp.cos(phases), -jnp.sin(phases)]) / NLON).astype(jnp.bfloat16)
    seg_width = NLON // N_LON
    tend_blocks = jnp.transpose(tendency.reshape(F, NLAT, N_LON, seg_width), (2, 0, 1, 3))
    back_blocks = jnp.transpose(back_table.reshape(2, PAIRS, 2, N_LON, seg_width), (3, 0, 1, 2, 4))

    def add_segment(running, inputs):
        tend_piece, back_piece = inputs
        segment = jnp.einsum('flx,rpqx->pqfrl', tend_piece.astype(jnp.float32), back_piece.astype(jnp.float32))
        segment = lax.optimization_barrier(segment.astype(jnp.bfloat16)).astype(jnp.float32)
        return (running + segment, None)
    analysis, _ = lax.scan(add_segment, jnp.zeros((PAIRS, 2, F, 2, NLAT), jnp.float32), (tend_blocks, back_blocks))
    fan = (analysis * kept_mask[:, :, None, None, :]).astype(jnp.bfloat16)
    down_scale = math.sqrt(M)

    def direct_slot(inputs):
        basis, values, part_one, part_two, signs = inputs
        north_half = values[..., :half_lats]
        south_half = jnp.flip(values[..., half_lats:], axis=-1)
        mixed_terms = jnp.stack([north_half, south_half], axis=1).astype(jnp.float32)
        products = jnp.einsum('qhfrk,ck->qhfrc', mixed_terms, basis.astype(jnp.float32))
        result_cols = part_one * (products[0, 0] + signs * products[0, 1]) + part_two * (products[1, 0] + signs * products[1, 1])
        return result_cols * down_scale
    spectral_tendency = lax.map(direct_slot, (legendre, fan, first_part, second_part, parity))
    spectral_tendency = jnp.transpose(spectral_tendency, (1, 2, 0, 3))
    valid_cols = first_part + second_part
    divisor = 1.0 + helm_coef[:, None, None, None] * (degree * (degree + 1.0))[None, None]
    spec_new = valid_cols[None, None] * (spec + spectral_tendency) / divisor
    return (grid_field, spec_new)
```

```python
import math

import jax
import jax.numpy as jnp
import numpy as np
from jax import lax
from jax.experimental import pallas as pl
from jax.experimental.pallas import tpu as pltpu
from jax.sharding import PartitionSpec as P

M = 1280
NLON = 5120
SEG = 320
MESH = pl.DeviceIdType.MESH
F32, BF16, I32 = jnp.float32, jnp.bfloat16, jnp.int32


def tables():
    x = np.arange(SEG)
    a = np.arange(40)
    psi = 2 * np.pi * ((a[None, :] * x[:, None]) % SEG) / SEG
    cos_ax, sin_ax = np.cos(psi), np.sin(psi)

    def alpha(b, q):
        m = np.where(q == 0, b, M - 1 - b)
        return 2 * np.pi * ((m[None, :] * x[:, None]) % NLON) / NLON

    t2rep = np.zeros((640, 256))
    t2rep[:, :240] = np.tile(np.concatenate([cos_ax, sin_ax]), (1, 6))
    lane = np.arange(240)
    b6, r, i, q = lane // 40, lane % 40 // 20, lane % 20 // 2, lane % 2
    twa, twb = np.zeros((3, SEG, 256)), np.zeros((3, SEG, 256))
    w1, w2 = np.zeros((3, 240, 256)), np.zeros((3, 240, 256))
    col = np.arange(256)
    d, icol = col // 16, col % 16
    for g in range(3):
        b = 6 * g + b6
        ok = b < 16
        twa[g, :, :240] = np.cos(alpha(b, q)) * ok
        twb[g, :, :240] = np.sin(alpha(b, q)) * ok
        bq = np.where(q == 0, b, 15 - b)
        beta = 2 * np.pi * ((bq[:, None] * d[None, :]) % 16) / 16
        same = (i[:, None] == icol[None, :]) * ok[:, None] * 2.0
        w1[g] = same * np.where(r[:, None] == 0, np.cos(beta), -np.sin(beta))
        w2[g] = same * np.where(r[:, None] == 0, -np.sin(beta), -np.cos(beta))
    rep = np.zeros((3, 128, 256))
    for s3 in range(3):
        rep[s3, 40 * s3 + lane % 40, lane] = 1.0
    ca = np.concatenate([t2rep, *twa, *twb, *w1, *w2, *rep])
    lane = np.arange(512)
    b, i, q = lane // 32, lane % 32 // 2, lane % 2
    ok = lane % 32 < 20
    bq = np.where(q == 0, b, 15 - b)
    beta = 2 * np.pi * ((bq[None, :] * d[:, None]) % 16) / 16
    same = (i[None, :] == icol[:, None]) * ok[None, :] * 1.0
    cb = np.concatenate(
        [same * np.cos(beta), -same * np.sin(beta), np.cos(alpha(b, q)) * ok, np.sin(alpha(b, q)) * ok]
    )
    cc = np.concatenate([cos_ax.T, sin_ax.T])
    svec = np.full((2, 16, 512), -1, np.int32)
    s2vec = np.full((2, 8, M), -1, np.int32)
    for core in range(2):
        for i in range(10):
            line = i if core == 0 else 9 - i
            for rho in range(40):
                s, r, q = rho // 4, rho % 4 // 2, rho % 2
                target = s // 3 * 128 + s % 3 * 40 + r * 20 + line * 2 + q
                svec[core, i, target] = rho
                s2vec[core, :, i * 128 + rho] = target
    return [jnp.asarray(t, BF16) for t in (ca, cb, cc)] + [jnp.asarray(svec), jnp.asarray(s2vec)]


T2, TWA, TWB, W1, W2, REP = 0, 640, 1600, 2560, 3280, 4000


def band_of(lat, half, hemi):
    z, y = lat // 8, lat % 8
    even = jnp.where(hemi == 0, 2 * half, 6 - 2 * half)
    delta = (z - even + 8) % 8
    near = jnp.logical_and(delta >= 1, delta <= 4)
    band = jnp.where(near, even + 1, even) * 8 + y
    quarter = jnp.where(near, delta - 1, (8 - delta) % 8)
    return band, quarter


def block_of(lat, half, hemi):
    band, quarter = band_of(lat, half, hemi)
    north = jnp.where(hemi == 0, band, 63 - band)
    return 4 * (north - 16 * half) + jnp.where(hemi == 0, quarter, 3 - quarter)


def owner_of(band, quarter, field):
    hemi = band // 32
    north = jnp.where(hemi == 0, band, 63 - band)
    z, y = band // 8, band % 8
    z = (z + jnp.where(z % 2 == 1, quarter, 8 - quarter)) % 8
    return z * 8 + y, 2 * (4 * (north // 16) + field) + hemi


def iota(shape, dim):
    return lax.broadcasted_iota(I32, shape, dim)


def dot(x, y):
    return jnp.dot(x, y, preferred_element_type=F32)


def kernel(
    mix, leg, fsend, rwx, wrow, wcol, ca, cb, cc, svec, s2vec, fac, sel, spec_t, mul_t,
    grid_out, spec_out,
    cav, cbv, ccv, part, prcv, summ, xrcv, xt, tt, smat, s2m, oht, oh, bbuf, brcv, frcv, rwrcv,
    bd, gbuf, grcv, abuf, ebuf, ercv, fall,
    csem, psem, fs, fr, xs, xr, bs, br, es, er, gs, gr, as_, ar, ws, wr,
):
    lat, lon = lax.axis_index("lat"), lax.axis_index("lon")
    chip, core = lon // 2, lon % 2
    half, field = chip // 4, chip % 4
    partner = 2 * chip + 1 - core
    band, quarter = band_of(lat, half, core)

    barrier = pltpu.get_barrier_semaphore()

    def greet(to_lat, to_lon):
        pl.semaphore_signal(barrier, inc=1, device_id=(to_lat, to_lon), device_id_type=MESH)

    greet(lat, partner)

    @pl.loop(1, 8)
    def _(t):
        greet(lat, 2 * ((chip + t) % 8) + core)

    @pl.loop(0, 16)
    def _(n):
        to_lat, to_lon = owner_of(lat, n // 4, n % 4)

        @pl.when(jnp.logical_or(to_lat != lat, to_lon != lon))
        def _():
            greet(to_lat, to_lon)

        @pl.when(jnp.logical_or(band != lat, n != lon))
        def _():
            greet(band, n)

    @pl.loop(1, 64)
    def _(t):
        greet((lat + t) % 64, lon)

    consts = [
        pltpu.make_async_copy(src, dst, csem.at[n])
        for n, (src, dst) in enumerate([(ca, cav), (cb, cbv), (cc, ccv)])
    ]
    for copy in consts:
        copy.start()

    @pl.loop(0, 5)
    def _(sp):
        terms = dot(mix[2 * sp], leg[2 * sp]) + dot(mix[2 * sp + 1], leg[2 * sp + 1])
        terms = (terms * (0.5 / math.sqrt(M))).astype(BF16)
        part[:, :, sp] = terms.reshape(2, 4, 8, M)

    my_slot_lat, my_slot_lon = owner_of(lat, 0, field)
    is_self = jnp.logical_and(my_slot_lat == lat, my_slot_lon == lon)
    pl.semaphore_wait(barrier, 103 - 2 * is_self.astype(I32))

    swap = pltpu.make_async_remote_copy(
        part.at[1 - core], prcv, psem.at[0], psem.at[1], device_id=(lat, partner), device_id_type=MESH
    )
    swap.start()

    def forcing_copy(n):
        to_lat, to_lon = owner_of(lat, n // 4, n % 4)
        away = jnp.logical_or(to_lat != lat, to_lon != lon)
        src, dst = fsend.at[n % 4, n // 4], frcv.at[lon]
        remote = pltpu.make_async_remote_copy(
            src, dst, fs.at[n], fr.at[0], device_id=(to_lat, to_lon), device_id_type=MESH
        )
        return away, remote, pltpu.make_async_copy(src, dst, fr.at[0])

    def rows_copy():
        to_lat, to_lon = owner_of(lat, lon // 4, lon % 4)
        away = jnp.logical_or(to_lat != lat, to_lon != lon)
        remote = pltpu.make_async_remote_copy(
            rwx.at[lon // 4], rwrcv, ws, wr, device_id=(to_lat, to_lon), device_id_type=MESH
        )
        return away, remote, pltpu.make_async_copy(rwx.at[lon // 4], rwrcv, wr)

    def launch(away, remote, local):
        @pl.when(away)
        def _():
            remote.start()

        @pl.when(jnp.logical_not(away))
        def _():
            local.start()

    swap.wait_recv()
    summ[...] = (part[core].astype(F32) + prcv[...].astype(F32)).astype(BF16)

    def shared(which, to):
        return pltpu.make_async_remote_copy(
            summ.at[to % 4, :, :, pl.ds(pl.multiple_of(640 * (to // 4), 128), 640)],
            xrcv.at[which], xs.at[which], xr.at[which], device_id=(lat, 2 * to + core), device_id_type=MESH,
        )

    for t in (4, 3, 5, 2, 6, 1, 7):
        shared(t, (chip + t) % 8).start()

    @pl.loop(0, 16)
    def _(n):
        launch(*forcing_copy(n))

    launch(*rows_copy())

    lanes = iota((128, 512), 0)
    for i in range(10):
        smat[i] = (svec[core, i : i + 1, :] == lanes).astype(BF16)
    for s3 in range(3):
        oht[s3] = (wrow[s3, 0:1, :] == iota((640, 256), 0)).astype(BF16)
    for t in range(5):
        oh[:, 128 * t : 128 * t + 128] = (wcol[...] == iota((768, 128), 1) + 128 * t).astype(BF16)
    s2m[...] = (s2vec[core, 0:1, :] == iota((512, M), 0)).astype(BF16)

    total = summ[field, :, :, pl.ds(pl.multiple_of(640 * half, 128), 640)].astype(F32)
    for t in (1, 7, 2, 6, 3, 5, 4):
        shared(t, (chip + t) % 8).wait_recv()
        total = total + xrcv[t].astype(F32)
    xt[0:40, :] = total.reshape(40, 640)
    xt[40:128, :] = jnp.zeros((88, 640), F32)
    tt[...] = xt[...].T
    packed = dot(tt[pl.ds(0, 64, stride=10), :].astype(BF16), smat[0])
    for i in range(1, 10):
        packed += dot(tt[pl.ds(i, 64, stride=10), :].astype(BF16), smat[i])
    for j in range(4):
        bbuf[:, j, :] = packed[:, 128 * j : 128 * j + 128]

    def to_lines(t):
        to = (lat + t) % 64
        return pltpu.make_async_remote_copy(
            bbuf.at[block_of(to, half, core)], brcv.at[lat], bs, br, device_id=(to, lon), device_id_type=MESH
        )

    @pl.loop(1, 64)
    def _(t):
        to_lines(t).start()

    pltpu.make_async_copy(bbuf.at[block_of(lat, half, core)], brcv.at[lat], br).start()
    pltpu.make_async_copy(frcv, frcv, fr.at[0]).wait()
    push = frcv[...].astype(F32).reshape(256, SEG).T
    pltpu.make_async_copy(rwrcv, rwrcv, wr).wait()
    for copy in consts:
        copy.wait()
    pltpu.make_async_copy(brcv, brcv, br).wait()

    rows = jnp.concatenate([brcv[:, j, :].astype(BF16) for j in range(4)], axis=0)
    coef = jnp.zeros((640, 240), F32)
    for s3 in range(3):
        spread = dot(rows, cav[REP + 128 * s3 : REP + 128 * s3 + 128, :240]).astype(BF16)
        coef += dot(oht[s3], spread)
    lane = iota((40, 240), 1)
    for b in range(16):
        m = iota((40, 240), 0) * 16 + b
        m = jnp.where(lane % 2 == 1, M - 1 - m, m)
        low = 40 * (b % 6)
        keep = jnp.logical_and(lane >= low, lane < low + 40)
        keep = jnp.logical_and(keep, m.astype(F32) < rwrcv[0:1, 0:240])
        value = jnp.where(keep, coef[40 * b : 40 * b + 40], 0.0)
        if b == 0:
            value = jnp.where(m == 0, 0.5 * value, value)
        bd[40 * b : 40 * b + 40, :] = value.astype(BF16)

    sign = jnp.where(iota((1, 240), 1) % 2 == 1, -1.0, 1.0)
    y = jnp.zeros((SEG, 256), F32)
    for g, depth in enumerate((240, 240, 160)):
        cs = dot(cav[T2 : T2 + 640, :depth], bd[240 * g : 240 * g + depth, :])
        c, s = cs[:SEG], cs[SEG:] * sign
        ta = cav[TWA + SEG * g : TWA + SEG * g + SEG, :240].astype(F32)
        tb = cav[TWB + SEG * g : TWB + SEG * g + SEG, :240].astype(F32)
        y += dot((ta * c - tb * s).astype(BF16), cav[W1 + 240 * g : W1 + 240 * g + 240, :])
        y += dot((tb * c + ta * s).astype(BF16), cav[W2 + 240 * g : W2 + 240 * g + 240, :])
    tend = (push - 0.5 * y * y).astype(BF16)
    gbuf[...] = y.T.astype(BF16).reshape(16, 16, SEG)

    gc, gi = dot(tend, cbv[0:256, :]), dot(tend, cbv[256:512, :])
    ta, tb = cbv[512:832, :].astype(F32), cbv[832:1152, :].astype(F32)
    kc = dot(ccv[...], (ta * gc + tb * gi).astype(BF16))
    ks = dot(ccv[...], (ta * gi - tb * gc).astype(BF16))
    lane = iota((40, 512), 1)
    sign = jnp.where(lane % 2 == 1, -1.0, 1.0)
    m = iota((40, 512), 0) * 16 + lane // 32
    m = jnp.where(lane % 2 == 1, M - 1 - m, m)
    scale = jnp.where(m.astype(F32) < rwrcv[0:1, 256:768], 1.0 / NLON, 0.0)
    real = (kc[:40] + sign * ks[40:]) * scale
    imag = (ks[:40] - sign * kc[40:]) * scale
    lane = iota((40, 128), 1)
    for b in range(16):
        tile, off = 128 * (b // 4), 32 * (b % 4)
        re, im = real[:, tile : tile + 128], imag[:, tile : tile + 128]
        re = pltpu.roll(re, (128 - off) % 128, 1) if off else re
        im = pltpu.roll(im, (148 - off) % 128, 1)
        value = jnp.where(lane < 20, re, jnp.where(lane < 40, im, 0.0))
        abuf[0, 40 * b : 40 * b + 40, :] = value.astype(BF16)
        abuf[1, 40 * b : 40 * b + 40, :] = pltpu.roll(value, 40, 1).astype(BF16)
        abuf[2, 40 * b : 40 * b + 40, :] = pltpu.roll(value, 80, 1).astype(BF16)
    back = jnp.zeros((256, 128), F32)
    for s3 in range(3):
        back += dot(oh[256 * s3 : 256 * s3 + 256, :], abuf[s3])
    for j in range(4):
        ebuf[:, j, :] = back[64 * j : 64 * j + 64]

    block = block_of(lat, half, core)

    def to_waves(t):
        to = (lat + t) % 64
        return pltpu.make_async_remote_copy(
            ebuf.at[to], ercv.at[block], es, er, device_id=(to, lon), device_id_type=MESH
        )

    @pl.loop(1, 64)
    def _(t):
        to_waves(t).start()

    pltpu.make_async_copy(ebuf.at[lat], ercv.at[block], er).start()

    def grid_copy(n):
        away = jnp.logical_or(band != lat, n != lon)
        src, dst = gbuf.at[n], grcv.at[field, quarter]
        remote = pltpu.make_async_remote_copy(
            src, dst, gs.at[n], gr, device_id=(band, n), device_id_type=MESH
        )
        return away, remote, pltpu.make_async_copy(src, dst, gr)

    @pl.loop(0, 16)
    def _(n):
        launch(*grid_copy(n))

    pltpu.make_async_copy(ercv, ercv, er).wait()
    rows = jnp.concatenate([ercv[:, j, :].astype(BF16) for j in range(4)], axis=1)
    placed = dot(rows, s2m[...])
    for i in range(10):
        tt[pl.ds(i, 64, stride=10), :] = placed[:, 128 * i : 128 * i + 128]
    xt[...] = tt[...].T
    fall[core, chip] = xt[0:40, :].astype(BF16).reshape(5, 8, 640)

    def around(t):
        to = (chip + t) % 8
        return pltpu.make_async_remote_copy(
            fall.at[core, chip], fall.at[core, chip], as_.at[t], ar.at[t],
            device_id=(lat, 2 * to + core), device_id_type=MESH,
        )

    def across(t):
        which = (chip + 8 - t) % 8
        return pltpu.make_async_remote_copy(
            fall.at[core, which], fall.at[core, which], as_.at[8 + t], ar.at[8 + t],
            device_id=(lat, partner), device_id_type=MESH,
        )

    for t in (4, 3, 5, 2, 6, 1, 7):
        around(t).start()
    across(0).start()
    for t in (1, 7, 2, 6, 3, 5, 4):
        pltpu.make_async_copy(fall.at[core, 0], fall.at[core, 0], ar.at[t]).wait()
        across(t).start()
    for t in range(8):
        across(t).wait_recv()

    nt = (((1,), (1,)), ((), ()))

    @pl.loop(0, 5)
    def _(sp):
        lows, highs = fall[:, 0:4, sp], fall[:, 4:8, sp]
        low = lows.astype(F32).reshape(64, 640).astype(BF16)
        high = highs.astype(F32).reshape(64, 640).astype(BF16)
        for s2 in range(2):
            basis = leg[2 * sp + s2]
            sums = lax.dot_general(low, basis[:, :640], nt, preferred_element_type=F32)
            sums += lax.dot_general(high, basis[:, 640:], nt, preferred_element_type=F32)
            sums = sums * fac[2 * sp + s2]
            folded = jnp.dot(sel[...], sums, preferred_element_type=F32, precision=lax.Precision.HIGHEST)
            spec_out[2 * sp + s2] = (spec_t[2 * sp + s2] + folded) * mul_t[2 * sp + s2]

    pltpu.make_async_copy(grcv, grcv, gr).wait()
    for f in range(4):
        for w in range(4):
            grid_out[f, 10 * w : 10 * w + 10, :] = grcv[f, w].astype(F32)[:10]

    swap.wait_send()
    for t in range(1, 8):
        shared(t, (chip + t) % 8).wait_send()
        around(t).wait_send()
    for t in range(8):
        across(t).wait_send()
    rest = brcv.at[pl.ds(0, 63)]
    pltpu.make_async_copy(rest, rest, bs).wait()
    pltpu.make_async_copy(rest, rest, es).wait()

    @pl.loop(0, 16)
    def _(n):
        away, remote, _ = forcing_copy(n)

        @pl.when(away)
        def _():
            remote.wait_send()

        away, remote, _ = grid_copy(n)

        @pl.when(away)
        def _():
            remote.wait_send()

    away, remote, _ = rows_copy()

    @pl.when(away)
    def _():
        remote.wait_send()


def body(spec, legendre, wave_pairs, row_waves, forcing, helm_coef):
    lat_id, lon_id = lax.axis_index("lat"), lax.axis_index("lon")
    v = lax.dynamic_slice_in_dim(wave_pairs, lat_id * 10, 10)[:, None]
    col = (lon_id * 84 + jnp.arange(84, dtype=I32))[None, :]
    edge = M - v
    first = col < edge
    valid = col < M + 1
    second = jnp.logical_and(valid, jnp.logical_not(first))
    offset = jnp.where(first, col, col - edge)
    parity = (1 - 2 * (offset % 2)).astype(F32)
    degree = jnp.where(first, v + col, col - 1).astype(F32)

    parts = jnp.stack([first, second], axis=1).astype(F32)[:, None, None, None, None]
    signs = jnp.stack([jnp.ones_like(parity), parity], axis=1)[:, :, None, None, None, None]
    slot = (jnp.arange(10)[:, None] % 2 == jnp.arange(2)[None, :]).astype(F32)
    factor = parts * signs * slot[:, None, None, :, None, None, None]
    spec_t = jnp.transpose(spec, (2, 0, 1, 3))
    mix = factor * spec_t.astype(BF16).astype(F32)[:, None, :, None, :, None]
    mix = mix.astype(BF16).reshape(10, 64, 84)
    fac = jnp.broadcast_to(factor * math.sqrt(M), (10, 2, 4, 2, 2, 2, 84)).reshape(10, 64, 84)
    row = np.arange(64)
    sel = jnp.asarray((row[None, :] // 8 % 4 * 2 + row[None, :] // 2 % 2) == np.arange(8)[:, None], F32)
    divisor = 1.0 + helm_coef[None, :, None] * (degree * (degree + 1.0))[:, None, :]
    mul_t = valid.astype(F32)[:, None, :] / divisor
    mul_t = jnp.broadcast_to(mul_t[:, :, None], (10, 4, 2, 84)).reshape(10, 8, 84)

    fsend = forcing.astype(BF16).reshape(4, 4, 10, SEG)
    fsend = jnp.pad(fsend, ((0, 0), (0, 0), (0, 6), (0, 0)))
    limits = jnp.repeat(row_waves.astype(F32).reshape(4, 10), 2, axis=1)
    rwx = jnp.concatenate(
        [
            jnp.pad(jnp.tile(limits, (1, 12)), ((0, 0), (0, 16))),
            jnp.tile(jnp.pad(limits, ((0, 0), (0, 12))), (1, 16)),
        ],
        axis=1,
    )
    rwx = jnp.broadcast_to(rwx[:, None], (4, 8, 768))
    place = (wave_pairs % 16 * 40 + wave_pairs // 16).reshape(64, 10)
    place = jnp.pad(place, ((0, 0), (0, 2)), constant_values=-1).reshape(64, 4, 3)
    place = jnp.transpose(place, (2, 1, 0)).reshape(3, 256)
    wrow = jnp.broadcast_to(place[:, None], (3, 8, 256))
    wcol = jnp.broadcast_to(place.reshape(768, 1), (768, 128))

    ca, cb, cc, svec, s2vec = tables()
    vmem, hbm = pl.BlockSpec(memory_space=pltpu.VMEM), pl.BlockSpec(memory_space=pl.ANY)
    dma = pltpu.SemaphoreType.DMA
    grid_field, spec_new = pl.pallas_call(
        kernel,
        out_shape=(
            jax.ShapeDtypeStruct((4, 40, SEG), F32),
            jax.ShapeDtypeStruct((10, 8, 84), F32),
        ),
        in_specs=[vmem] * 6 + [hbm] * 3 + [vmem] * 6,
        out_specs=(vmem, vmem),
        scratch_shapes=[
            pltpu.VMEM((4384, 256), BF16), pltpu.VMEM((1152, 512), BF16), pltpu.VMEM((80, SEG), BF16),
            pltpu.VMEM((2, 4, 5, 8, M), BF16), pltpu.VMEM((4, 5, 8, M), BF16), pltpu.VMEM((4, 5, 8, M), BF16),
            pltpu.VMEM((8, 5, 8, 640), BF16), pltpu.VMEM((128, 640), F32), pltpu.VMEM((640, 128), F32),
            pltpu.VMEM((10, 128, 512), BF16), pltpu.VMEM((512, M), BF16), pltpu.VMEM((3, 640, 256), BF16),
            pltpu.VMEM((768, 640), BF16), pltpu.VMEM((64, 4, 128), F32), pltpu.VMEM((64, 4, 128), F32),
            pltpu.VMEM((16, 16, SEG), BF16), pltpu.VMEM((8, 768), F32), pltpu.VMEM((640, 240), BF16),
            pltpu.VMEM((16, 16, SEG), BF16), pltpu.VMEM((4, 4, 16, SEG), BF16), pltpu.VMEM((3, 640, 128), BF16),
            pltpu.VMEM((64, 4, 128), F32), pltpu.VMEM((64, 4, 128), F32), pltpu.VMEM((2, 8, 5, 8, 640), BF16),
            dma((3,)), dma((2,)), dma((16,)), dma((1,)), dma((8,)), dma((8,)), dma, dma, dma, dma,
            dma((16,)), dma, dma((16,)), dma((16,)), dma, dma,
        ],
        compiler_params=pltpu.CompilerParams(
            collective_id=0, has_side_effects=True, vmem_limit_bytes=60 * 1024 * 1024
        ),
        name="step",
    )(mix, legendre, fsend, rwx, wrow, wcol, ca, cb, cc, svec, s2vec, fac, sel, spec_t.reshape(10, 8, 84), mul_t)
    spec_new = jnp.transpose(spec_new.reshape(10, 4, 2, 84), (1, 2, 0, 3))
    return (grid_field, spec_new)


def solution(mesh):
    return jax.shard_map(
        body,
        mesh=mesh,
        in_specs=(
            P(None, None, "lat", "lon"),
            P("lat", "lon", None),
            P(),
            P("lat"),
            P(None, "lat", "lon"),
            P(),
        ),
        out_specs=(P(None, "lat", "lon"), P(None, None, "lat", "lon")),
        check_vma=False,
    )
```

```python
import math

import jax
import jax.numpy as jnp
import numpy as np
from jax import lax
from jax.experimental import pallas as pl
from jax.experimental.pallas import tpu as pltpu
from jax.sharding import PartitionSpec as P

M = 1280
NLON = 5120
SEG = 320
MESH = pl.DeviceIdType.MESH
F32, BF16, I32 = jnp.float32, jnp.bfloat16, jnp.int32


def tables():
    x = np.arange(SEG)
    a = np.arange(40)
    psi = 2 * np.pi * ((a[None, :] * x[:, None]) % SEG) / SEG
    cos_ax, sin_ax = np.cos(psi), np.sin(psi)

    def alpha(b, q):
        m = np.where(q == 0, b, M - 1 - b)
        return 2 * np.pi * ((m[None, :] * x[:, None]) % NLON) / NLON

    t2rep = np.zeros((640, 256))
    t2rep[:, :240] = np.tile(np.concatenate([cos_ax, sin_ax]), (1, 6))
    base = np.zeros((640, 256))
    slot = np.arange(32)
    base[:, :32] = np.concatenate([np.cos(alpha(slot // 2, slot % 2)), np.sin(alpha(slot // 2, slot % 2))])
    lane = np.arange(240)
    b6, r, i, q = lane // 40, lane % 40 // 20, lane % 20 // 2, lane % 2
    w1, w2 = np.zeros((3, 240, 256)), np.zeros((3, 240, 256))
    col = np.arange(256)
    d, icol = col // 16, col % 16
    vecs = np.full((8, M), -1, np.int32)
    for g in range(3):
        b = 6 * g + b6
        ok = b < 16
        vecs[0, 256 * g : 256 * g + 240] = np.where(ok, 2 * b + q, -1)
        bq = np.where(q == 0, b, 15 - b)
        beta = 2 * np.pi * ((bq[:, None] * d[None, :]) % 16) / 16
        same = (i[:, None] == icol[None, :]) * ok[:, None] * 2.0
        w1[g] = same * np.where(r[:, None] == 0, np.cos(beta), -np.sin(beta))
        w2[g] = same * np.where(r[:, None] == 0, -np.sin(beta), -np.cos(beta))
    rep = np.zeros((3, 128, 256))
    for s3 in range(3):
        rep[s3, 40 * s3 + lane % 40, lane] = 1.0
    ca = np.concatenate([t2rep, base, *w1, *w2, *rep])
    vecs[2, :240] = i
    vecs[2, 240:768] = -1000
    lane = np.arange(512)
    b, i, q = lane // 32, lane % 32 // 2, lane % 2
    ok = lane % 32 < 20
    vecs[0, 768:] = np.where(ok, 2 * b + q, -1)
    vecs[2, 256:768] = np.where(ok, i, -1000)
    bq = np.where(q == 0, b, 15 - b)
    beta = 2 * np.pi * ((bq[None, :] * d[:, None]) % 16) / 16
    same = (i[None, :] == icol[:, None]) * ok[None, :] * 1.0
    cb = np.concatenate([same * np.cos(beta), -same * np.sin(beta)])
    cc = np.concatenate([cos_ax.T, sin_ax.T])
    lane = np.arange(768)
    s = 3 * (lane % 256 // 64) + lane // 256
    vecs[1, :768] = np.where(s < 10, 10 * (lane % 64) + s, -1)
    svec = np.full((2, 16, 512), -1, np.int32)
    s2vec = np.full((2, 8, M), -1, np.int32)
    for core in range(2):
        for i in range(10):
            line = i if core == 0 else 9 - i
            for rho in range(40):
                s, r, q = rho // 4, rho % 4 // 2, rho % 2
                target = s // 3 * 128 + s % 3 * 40 + r * 20 + line * 2 + q
                svec[core, i, target] = rho
                s2vec[core, :, i * 128 + rho] = target
    return [jnp.asarray(t, BF16) for t in (ca, cb, cc)] + [jnp.asarray(t) for t in (svec, s2vec, vecs)]


T2, BASE, W1, W2, REP = 0, 640, 1280, 2000, 2720


def band_of(lat, half, hemi):
    z, y = lat // 8, lat % 8
    even = jnp.where(hemi == 0, 2 * half, 6 - 2 * half)
    delta = (z - even + 8) % 8
    near = jnp.logical_and(delta >= 1, delta <= 4)
    band = jnp.where(near, even + 1, even) * 8 + y
    quarter = jnp.where(near, delta - 1, (8 - delta) % 8)
    return band, quarter


def block_of(lat, half, hemi):
    band, quarter = band_of(lat, half, hemi)
    north = jnp.where(hemi == 0, band, 63 - band)
    return 4 * (north - 16 * half) + jnp.where(hemi == 0, quarter, 3 - quarter)


def owner_of(band, quarter, field):
    hemi = band // 32
    north = jnp.where(hemi == 0, band, 63 - band)
    z, y = band // 8, band % 8
    z = (z + jnp.where(z % 2 == 1, quarter, 8 - quarter)) % 8
    return z * 8 + y, 2 * (4 * (north // 16) + field) + hemi


def iota(shape, dim):
    return lax.broadcasted_iota(I32, shape, dim)


def dot(x, y):
    return jnp.dot(x, y, preferred_element_type=F32)


def kernel(
    spec, leg_hbm, pairs_s, pairs, limits, forcing_hbm, helm, ca, cb, cc, svec, s2vec, vecs,
    grid_out, spec_out,
    leg, forcing, cav, cbv, ccv, spec_t, mix, fac, mul_t, fpad, fsend, rwx, part, prcv, summ, xrcv, xsum,
    xt, tt, smat, s2m, oht, oh, texp, bbuf, brcv, frcv, rwrcv, bd, gbuf, grcv, gout, abuf, ebuf, ercv, fall,
    csem, psem, fs, fr, xs, xr, bs, br, es, er, gs, gr, as_, ar, ws, wr,
):
    lat, lon = lax.axis_index("lat"), lax.axis_index("lon")
    chip, core = lon // 2, lon % 2
    half, field = chip // 4, chip % 4
    partner = 2 * chip + 1 - core
    band, quarter = band_of(lat, half, core)

    barrier = pltpu.get_barrier_semaphore()

    def greet(to_lat, to_lon):
        pl.semaphore_signal(barrier, inc=1, device_id=(to_lat, to_lon), device_id_type=MESH)

    greet(lat, partner)

    @pl.loop(1, 8)
    def _(t):
        greet(lat, 2 * ((chip + t) % 8) + core)

    @pl.loop(0, 16)
    def _(n):
        to_lat, to_lon = owner_of(lat, n // 4, n % 4)

        @pl.when(jnp.logical_or(to_lat != lat, to_lon != lon))
        def _():
            greet(to_lat, to_lon)

        @pl.when(jnp.logical_or(band != lat, n != lon))
        def _():
            greet(band, n)

    @pl.loop(1, 64)
    def _(t):
        greet((lat + t) % 64, lon)

    loads = [
        pltpu.make_async_copy(src, dst, csem.at[n])
        for n, (src, dst) in enumerate(
            [(leg_hbm, leg), (forcing_hbm, forcing), (ca, cav), (cb, cbv), (cc, ccv)]
        )
    ]
    for copy in loads:
        copy.start()

    row, col = iota((64, 84), 0), iota((64, 84), 1) + lon * 84
    second_wave, hemi_row = row % 2 == 1, row // 32 == 1
    pick = (row[:, :8] // 8 % 4 * 2 + row[:, :8] // 2 % 2 == iota((64, 8), 1)).astype(F32)
    low_col = iota((8, 84), 1) + lon * 84
    field_row = iota((8, 84), 0) // 2
    helm_row = jnp.full((8, 84), helm[3])
    for f in range(3):
        helm_row = jnp.where(field_row == f, helm[f], helm_row)

    @pl.loop(0, 10)
    def _(s):
        v = pairs_s[10 * lat + s]
        for f in range(4):
            spec_t[s, 2 * f : 2 * f + 2, :] = spec[f, s]
        edge = M - v
        first = col < edge
        second = jnp.logical_and(col < M + 1, jnp.logical_not(first))
        odd = jnp.where(first, col, col - edge) % 2 == 1
        used = jnp.logical_or(
            jnp.logical_and(second_wave, second), jnp.logical_and(jnp.logical_not(second_wave), first)
        )
        used = jnp.logical_and(used, row // 4 % 2 == s % 2)
        factor = jnp.where(used, jnp.where(jnp.logical_and(hemi_row, odd), -1.0, 1.0), 0.0)
        rounded = spec_t[s].astype(BF16).astype(F32)
        mix[s] = (factor * dot(pick, rounded)).astype(BF16)
        fac[s] = factor * math.sqrt(M)
        degree = jnp.where(low_col < edge, v + low_col, low_col - 1).astype(F32)
        valid = (low_col < M + 1).astype(F32)
        mul_t[s] = valid / (1.0 + helm_row * (degree * (degree + 1.0)))

    loads[0].wait()

    @pl.loop(0, 5)
    def _(sp):
        terms = dot(mix[2 * sp], leg[2 * sp]) + dot(mix[2 * sp + 1], leg[2 * sp + 1])
        terms = (terms * (0.5 / math.sqrt(M))).astype(BF16)
        part[:, :, sp] = terms.reshape(2, 4, 8, M)

    loads[1].wait()
    fpad[...] = jnp.zeros_like(fpad)
    for f in range(4):
        for w in range(4):
            fpad[f, w, 0:10, :] = forcing[f, 10 * w : 10 * w + 10, :]
    fsend[...] = fpad[...].astype(BF16)
    rwx[...] = jnp.zeros_like(rwx)
    rwx[:, 0:40] = jnp.broadcast_to(limits[...].astype(F32), (8, 40))

    my_slot_lat, my_slot_lon = owner_of(lat, 0, field)
    is_self = jnp.logical_and(my_slot_lat == lat, my_slot_lon == lon)
    pl.semaphore_wait(barrier, 103 - 2 * is_self.astype(I32))

    swap = pltpu.make_async_remote_copy(
        part.at[1 - core], prcv, psem.at[0], psem.at[1], device_id=(lat, partner), device_id_type=MESH
    )
    swap.start()

    def forcing_copy(n):
        to_lat, to_lon = owner_of(lat, n // 4, n % 4)
        away = jnp.logical_or(to_lat != lat, to_lon != lon)
        src, dst = fsend.at[n % 4, n // 4], frcv.at[lon]
        remote = pltpu.make_async_remote_copy(
            src, dst, fs.at[n], fr.at[0], device_id=(to_lat, to_lon), device_id_type=MESH
        )
        return away, remote, pltpu.make_async_copy(src, dst, fr.at[0])

    def rows_copy():
        to_lat, to_lon = owner_of(lat, lon // 4, lon % 4)
        away = jnp.logical_or(to_lat != lat, to_lon != lon)
        remote = pltpu.make_async_remote_copy(
            rwx, rwrcv, ws, wr, device_id=(to_lat, to_lon), device_id_type=MESH
        )
        return away, remote, pltpu.make_async_copy(rwx, rwrcv, wr)

    def launch(away, remote, local):
        @pl.when(away)
        def _():
            remote.start()

        @pl.when(jnp.logical_not(away))
        def _():
            local.start()

    @pl.loop(0, 16)
    def _(n):
        launch(*forcing_copy(n))

    launch(*rows_copy())

    swap.wait_recv()
    summ[...] = (part[core].astype(F32) + prcv[...].astype(F32)).astype(BF16)

    step = jnp.where(core == 0, 1, 7)

    def chunk(to):
        return summ.at[to % 4, :, :, pl.ds(pl.multiple_of(640 * (to // 4), 128), 640)]

    def shared(slot, owner, via, src=None):
        src = chunk((chip + owner * step) % 8) if src is None else src
        to = (chip + via * step) % 8
        return pltpu.make_async_remote_copy(
            src, xrcv.at[slot], xs.at[slot], xr.at[slot],
            device_id=(lat, 2 * to + core), device_id_type=MESH,
        )

    opening = [shared(4, 4, 2), shared(3, 3, 1), shared(5, 5, 7), shared(1, 1, 1), shared(7, 7, 7)]
    for copy in opening:
        copy.start()

    lanes = iota((128, 512), 0)
    for i in range(10):
        smat[i] = (svec[core, i : i + 1, :] == lanes).astype(BF16)

    opening[1].wait_recv()
    opening[0].wait_recv()
    onward = chunk((chip + 2 * step) % 8)[...].astype(F32) + xrcv[3].astype(F32) + xrcv[4].astype(F32)
    xsum[0] = onward.astype(BF16)
    ahead = shared(2, 2, 2, xsum.at[0])
    ahead.start()
    opening[2].wait_recv()
    onward = chunk((chip + 6 * step) % 8)[...].astype(F32) + xrcv[5].astype(F32)
    xsum[1] = onward.astype(BF16)
    behind = shared(6, 6, 6, xsum.at[1])
    behind.start()

    expand = (vecs[0:1, :] == iota((128, M), 0)).astype(BF16)
    loads[2].wait()
    base = cav[BASE : BASE + 640, 0:128]
    texp[...] = dot(base, expand).astype(BF16)
    waves = jnp.broadcast_to(pairs[...], (16, 640))
    top = iota((16, 640), 0)
    waves = jnp.where(top == 0, waves // 16, jnp.where(top == 1, waves % 16, 0)).astype(F32).astype(BF16)
    where_from = vecs[1:2, 0:768]
    placed = dot(waves, (where_from == iota((640, 768), 0)).astype(BF16))
    place = jnp.where(where_from >= 0, 40.0 * placed[1:2] + placed[0:1], -1.0)
    for s3 in range(3):
        oht[s3] = (place[:, 256 * s3 : 256 * s3 + 256] == iota((640, 256), 0).astype(F32)).astype(BF16)
    for k in range(6):
        across_rows = jnp.broadcast_to(place[:, 128 * k : 128 * k + 128], (128, 128)).T
        for t in range(5):
            oh[128 * k : 128 * k + 128, 128 * t : 128 * t + 128] = (
                across_rows == (iota((128, 128), 1) + 128 * t).astype(F32)
            ).astype(BF16)
    s2m[...] = (s2vec[core, 0:1, :] == iota((512, M), 0)).astype(BF16)

    total = summ[field, :, :, pl.ds(pl.multiple_of(640 * half, 128), 640)].astype(F32)
    opening[3].wait_recv()
    opening[4].wait_recv()
    ahead.wait_recv()
    behind.wait_recv()
    for slot in (1, 7, 2, 6):
        total = total + xrcv[slot].astype(F32)
    xt[0:40, :] = total.reshape(40, 640)
    xt[40:128, :] = jnp.zeros((88, 640), F32)
    tt[...] = xt[...].T
    packed = dot(tt[pl.ds(0, 64, stride=10), :].astype(BF16), smat[0])
    for i in range(1, 10):
        packed += dot(tt[pl.ds(i, 64, stride=10), :].astype(BF16), smat[i])
    for j in range(4):
        bbuf[:, j, :] = packed[:, 128 * j : 128 * j + 128]

    def to_lines(t):
        to = (lat + t) % 64
        return pltpu.make_async_remote_copy(
            bbuf.at[block_of(to, half, core)], brcv.at[lat], bs, br, device_id=(to, lon), device_id_type=MESH
        )

    @pl.loop(1, 64)
    def _(t):
        to_lines(t).start()

    pltpu.make_async_copy(bbuf.at[block_of(lat, half, core)], brcv.at[lat], br).start()
    pltpu.make_async_copy(frcv, frcv, fr.at[0]).wait()
    push = frcv[...].astype(F32).reshape(256, SEG).T
    pltpu.make_async_copy(rwrcv, rwrcv, wr).wait()
    chosen = (iota((128, 768), 0) == vecs[2:3, 0:768] + 10 * quarter).astype(F32)
    bound = jnp.dot(rwrcv[...], chosen, preferred_element_type=F32, precision=lax.Precision.HIGHEST)
    loads[3].wait()
    loads[4].wait()
    pltpu.make_async_copy(brcv, brcv, br).wait()

    rows = jnp.concatenate([brcv[:, j, :].astype(BF16) for j in range(4)], axis=0)
    coef = jnp.zeros((640, 240), F32)
    for s3 in range(3):
        spread = dot(rows, cav[REP + 128 * s3 : REP + 128 * s3 + 128, :240]).astype(BF16)
        coef += dot(oht[s3], spread)
    lane = iota((40, 240), 1)
    for b in range(16):
        m = iota((40, 240), 0) * 16 + b
        m = jnp.where(lane % 2 == 1, M - 1 - m, m)
        low = 40 * (b % 6)
        keep = jnp.logical_and(lane >= low, lane < low + 40)
        keep = jnp.logical_and(keep, m.astype(F32) < bound[0:1, 0:240])
        value = jnp.where(keep, coef[40 * b : 40 * b + 40], 0.0)
        if b == 0:
            value = jnp.where(m == 0, 0.5 * value, value)
        bd[40 * b : 40 * b + 40, :] = value.astype(BF16)

    sign = jnp.where(iota((1, 240), 1) % 2 == 1, -1.0, 1.0)
    y = jnp.zeros((SEG, 256), F32)
    for g, depth in enumerate((240, 240, 160)):
        cs = dot(cav[T2 : T2 + 640, :depth], bd[240 * g : 240 * g + depth, :])
        c, s = cs[:SEG], cs[SEG:] * sign
        ta = texp[0:SEG, 256 * g : 256 * g + 240].astype(F32)
        tb = texp[SEG:640, 256 * g : 256 * g + 240].astype(F32)
        y += dot((ta * c - tb * s).astype(BF16), cav[W1 + 240 * g : W1 + 240 * g + 240, :])
        y += dot((tb * c + ta * s).astype(BF16), cav[W2 + 240 * g : W2 + 240 * g + 240, :])
    tend = (push - 0.5 * y * y).astype(BF16)
    gbuf[...] = y.T.astype(BF16).reshape(16, 16, SEG)

    gc, gi = dot(tend, cbv[0:256, :]), dot(tend, cbv[256:512, :])
    ta, tb = texp[0:SEG, 768:M].astype(F32), texp[SEG:640, 768:M].astype(F32)
    kc = dot(ccv[...], (ta * gc + tb * gi).astype(BF16))
    ks = dot(ccv[...], (ta * gi - tb * gc).astype(BF16))
    lane = iota((40, 512), 1)
    sign = jnp.where(lane % 2 == 1, -1.0, 1.0)
    m = iota((40, 512), 0) * 16 + lane // 32
    m = jnp.where(lane % 2 == 1, M - 1 - m, m)
    scale = jnp.where(m.astype(F32) < bound[0:1, 256:768], 1.0 / NLON, 0.0)
    real = (kc[:40] + sign * ks[40:]) * scale
    imag = (ks[:40] - sign * kc[40:]) * scale
    lane = iota((40, 128), 1)
    for b in range(16):
        tile, off = 128 * (b // 4), 32 * (b % 4)
        re, im = real[:, tile : tile + 128], imag[:, tile : tile + 128]
        re = pltpu.roll(re, (128 - off) % 128, 1) if off else re
        im = pltpu.roll(im, (148 - off) % 128, 1)
        value = jnp.where(lane < 20, re, jnp.where(lane < 40, im, 0.0))
        abuf[0, 40 * b : 40 * b + 40, :] = value.astype(BF16)
        abuf[1, 40 * b : 40 * b + 40, :] = pltpu.roll(value, 40, 1).astype(BF16)
        abuf[2, 40 * b : 40 * b + 40, :] = pltpu.roll(value, 80, 1).astype(BF16)
    back = jnp.zeros((256, 128), F32)
    for s3 in range(3):
        back += dot(oh[256 * s3 : 256 * s3 + 256, :], abuf[s3])
    for j in range(4):
        ebuf[:, j, :] = back[64 * j : 64 * j + 64]

    block = block_of(lat, half, core)

    def to_waves(t):
        to = (lat + t) % 64
        return pltpu.make_async_remote_copy(
            ebuf.at[to], ercv.at[block], es, er, device_id=(to, lon), device_id_type=MESH
        )

    @pl.loop(1, 64)
    def _(t):
        to_waves(t).start()

    pltpu.make_async_copy(ebuf.at[lat], ercv.at[block], er).start()

    def grid_copy(n):
        away = jnp.logical_or(band != lat, n != lon)
        src, dst = gbuf.at[n], grcv.at[field, quarter]
        remote = pltpu.make_async_remote_copy(
            src, dst, gs.at[n], gr, device_id=(band, n), device_id_type=MESH
        )
        return away, remote, pltpu.make_async_copy(src, dst, gr)

    @pl.loop(0, 16)
    def _(n):
        launch(*grid_copy(n))

    pltpu.make_async_copy(ercv, ercv, er).wait()
    rows = jnp.concatenate([ercv[:, j, :].astype(BF16) for j in range(4)], axis=1)
    placed = dot(rows, s2m[...])
    for i in range(10):
        tt[pl.ds(i, 64, stride=10), :] = placed[:, 128 * i : 128 * i + 128]
    xt[...] = tt[...].T
    fall[core, chip] = xt[0:40, :].astype(BF16).reshape(5, 8, 640)

    def held(k):
        return fall.at[core, (chip + 64 - k * step) % 8]

    def around(k, have):
        to = (chip + (k - have + 8) * step) % 8
        return pltpu.make_async_remote_copy(
            held(have), held(have), as_.at[k], ar.at[k], device_id=(lat, 2 * to + core), device_id_type=MESH
        )

    def across(k):
        return pltpu.make_async_remote_copy(
            held(k), held(k), as_.at[8 + k], ar.at[8 + k], device_id=(lat, partner), device_id_type=MESH
        )

    hops = {2: 0, 6: 0, 1: 0, 7: 0, 4: 2, 3: 2, 5: 6}

    def arrived(k):
        pltpu.make_async_copy(held(k), held(k), ar.at[k]).wait()

    for k in (2, 6, 1, 7):
        around(k, 0).start()
    across(0).start()
    arrived(2)
    around(4, 2).start()
    around(3, 2).start()
    across(2).start()
    arrived(6)
    around(5, 6).start()
    across(6).start()
    for k in (1, 7, 3, 5, 4):
        arrived(k)
        across(k).start()
    for k in range(8):
        pltpu.make_async_copy(held(k), held(k), ar.at[8 + k]).wait()

    nt = (((1,), (1,)), ((), ()))
    of_row = iota((8, 64), 1)
    fold = (of_row // 8 % 4 * 2 + of_row // 2 % 2 == iota((8, 64), 0)).astype(F32)

    @pl.loop(0, 5)
    def _(sp):
        lows, highs = fall[:, 0:4, sp], fall[:, 4:8, sp]
        low = lows.astype(F32).reshape(64, 640).astype(BF16)
        high = highs.astype(F32).reshape(64, 640).astype(BF16)
        for s2 in range(2):
            basis = leg[2 * sp + s2]
            sums = lax.dot_general(low, basis[:, :640], nt, preferred_element_type=F32)
            sums += lax.dot_general(high, basis[:, 640:], nt, preferred_element_type=F32)
            sums = sums * fac[2 * sp + s2]
            folded = jnp.dot(fold, sums, preferred_element_type=F32, precision=lax.Precision.HIGHEST)
            done = (spec_t[2 * sp + s2] + folded) * mul_t[2 * sp + s2]
            for f in range(4):
                spec_out[f, 2 * sp + s2] = done[2 * f : 2 * f + 2]

    pltpu.make_async_copy(grcv, grcv, gr).wait()
    for f in range(4):
        for w in range(4):
            gout[f, 10 * w : 10 * w + 10, :] = grcv[f, w].astype(F32)[:10]
    grid_out[...] = gout[...].astype(BF16)

    swap.wait_send()
    for copy in opening + [ahead, behind]:
        copy.wait_send()
    for k, have in hops.items():
        around(k, have).wait_send()
    for k in range(8):
        across(k).wait_send()
    rest = brcv.at[pl.ds(0, 63)]
    pltpu.make_async_copy(rest, rest, bs).wait()
    pltpu.make_async_copy(rest, rest, es).wait()

    @pl.loop(0, 16)
    def _(n):
        away, remote, _ = forcing_copy(n)

        @pl.when(away)
        def _():
            remote.wait_send()

        away, remote, _ = grid_copy(n)

        @pl.when(away)
        def _():
            remote.wait_send()

    away, remote, _ = rows_copy()

    @pl.when(away)
    def _():
        remote.wait_send()


def body(spec, legendre, wave_pairs, row_waves, forcing, helm_coef):
    vmem, hbm = pl.BlockSpec(memory_space=pltpu.VMEM), pl.BlockSpec(memory_space=pl.ANY)
    smem = pl.BlockSpec(memory_space=pltpu.SMEM)
    dma = pltpu.SemaphoreType.DMA

    def v16(*shape):
        return pltpu.VMEM(shape, BF16)

    def v32(*shape):
        return pltpu.VMEM(shape, F32)

    grid_field, spec_new = pl.pallas_call(
        kernel,
        out_shape=(
            jax.ShapeDtypeStruct((4, 40, SEG), BF16),
            jax.ShapeDtypeStruct((4, 10, 2, 84), F32),
        ),
        in_specs=[vmem, hbm, smem, vmem, vmem, hbm, smem, hbm, hbm, hbm, vmem, vmem, vmem],
        out_specs=(vmem, vmem),
        scratch_shapes=[
            v16(10, 84, M), v32(4, 40, SEG), v16(3104, 256), v16(512, 512), v16(80, SEG), v32(10, 8, 84),
            v16(10, 64, 84), v32(10, 64, 84), v32(10, 8, 84), v32(4, 4, 16, SEG), v16(4, 4, 16, SEG), v32(8, 128),
            v16(2, 4, 5, 8, M), v16(4, 5, 8, M), v16(4, 5, 8, M), v16(8, 5, 8, 640), v16(2, 5, 8, 640),
            v32(128, 640), v32(640, 128), v16(10, 128, 512), v16(512, M), v16(3, 640, 256), v16(768, 640),
            v16(640, M), v32(64, 4, 128), v32(64, 4, 128), v16(16, 16, SEG), v32(8, 128), v16(640, 240),
            v16(16, 16, SEG), v16(4, 4, 16, SEG), v32(4, 40, SEG), v16(3, 640, 128), v32(64, 4, 128),
            v32(64, 4, 128), v16(2, 8, 5, 8, 640),
            dma((5,)), dma((2,)), dma((16,)), dma((1,)), dma((8,)), dma((8,)), dma, dma, dma, dma,
            dma((16,)), dma, dma((16,)), dma((16,)), dma, dma,
        ],
        compiler_params=pltpu.CompilerParams(
            collective_id=0, has_side_effects=True, vmem_limit_bytes=60 * 1024 * 1024
        ),
        name="step",
    )(
        jnp.transpose(spec, (0, 2, 1, 3)), legendre, wave_pairs, wave_pairs.reshape(1, 640),
        row_waves.reshape(1, 40), forcing, helm_coef, *tables(),
    )
    return (grid_field.astype(F32), jnp.transpose(spec_new, (0, 2, 1, 3)))


def solution(mesh):
    return jax.shard_map(
        body,
        mesh=mesh,
        in_specs=(
            P(None, None, "lat", "lon"),
            P("lat", "lon", None),
            P(),
            P("lat"),
            P(None, "lat", "lon"),
            P(),
        ),
        out_specs=(P(None, "lat", "lon"), P(None, None, "lat", "lon")),
        check_vma=False,
    )
```

```python
import math

import jax
import jax.numpy as jnp
import numpy as np
from jax import lax
from jax.experimental import pallas as pl
from jax.experimental.pallas import tpu as pltpu
from jax.sharding import PartitionSpec as P

M = 1280
NLON = 5120
SEG = 320
MESH = pl.DeviceIdType.MESH
F32, BF16, I32 = jnp.float32, jnp.bfloat16, jnp.int32


def tables():
    x = np.arange(SEG)
    a = np.arange(40)
    psi = 2 * np.pi * ((a[None, :] * x[:, None]) % SEG) / SEG
    cos_ax, sin_ax = np.cos(psi), np.sin(psi)

    def alpha(b, q):
        m = np.where(q == 0, b, M - 1 - b)
        return 2 * np.pi * ((m[None, :] * x[:, None]) % NLON) / NLON

    t2rep = np.zeros((640, 256))
    t2rep[:, :240] = np.tile(np.concatenate([cos_ax, sin_ax]), (1, 6))
    base = np.zeros((640, 256))
    slot = np.arange(32)
    base[:, :32] = np.concatenate([np.cos(alpha(slot // 2, slot % 2)), np.sin(alpha(slot // 2, slot % 2))])
    lane = np.arange(240)
    b6, r, i, q = lane // 40, lane % 40 // 20, lane % 20 // 2, lane % 2
    w1, w2 = np.zeros((3, 240, 256)), np.zeros((3, 240, 256))
    col = np.arange(256)
    d, icol = col // 16, col % 16
    vecs = np.full((8, M), -1, np.int32)
    for g in range(3):
        b = 6 * g + b6
        ok = b < 16
        vecs[0, 256 * g : 256 * g + 240] = np.where(ok, 2 * b + q, -1)
        bq = np.where(q == 0, b, 15 - b)
        beta = 2 * np.pi * ((bq[:, None] * d[None, :]) % 16) / 16
        same = (i[:, None] == icol[None, :]) * ok[:, None] * 2.0
        w1[g] = same * np.where(r[:, None] == 0, np.cos(beta), -np.sin(beta))
        w2[g] = same * np.where(r[:, None] == 0, -np.sin(beta), -np.cos(beta))
    rep = np.zeros((3, 128, 256))
    for s3 in range(3):
        rep[s3, 40 * s3 + lane % 40, lane] = 1.0
    ca = np.concatenate([t2rep, base, *w1, *w2, *rep])
    vecs[2, :240] = i
    vecs[2, 240:768] = -1000
    lane = np.arange(512)
    b, i, q = lane // 32, lane % 32 // 2, lane % 2
    ok = lane % 32 < 20
    vecs[0, 768:] = np.where(ok, 2 * b + q, -1)
    vecs[2, 256:768] = np.where(ok, i, -1000)
    bq = np.where(q == 0, b, 15 - b)
    beta = 2 * np.pi * ((bq[None, :] * d[:, None]) % 16) / 16
    same = (i[None, :] == icol[:, None]) * ok[None, :] * 1.0
    cb = np.concatenate([same * np.cos(beta), -same * np.sin(beta)])
    cc = np.concatenate([cos_ax.T, sin_ax.T])
    lane = np.arange(768)
    s = 3 * (lane % 256 // 64) + lane // 256
    vecs[1, :768] = np.where(s < 10, 10 * (lane % 64) + s, -1)
    svec = np.full((2, 16, 512), -1, np.int32)
    s2vec = np.full((2, 8, M), -1, np.int32)
    for core in range(2):
        for i in range(10):
            line = i if core == 0 else 9 - i
            for rho in range(40):
                s, r, q = rho // 4, rho % 4 // 2, rho % 2
                target = s // 3 * 128 + s % 3 * 40 + r * 20 + line * 2 + q
                svec[core, i, target] = rho
                s2vec[core, :, i * 128 + rho] = target
    return [jnp.asarray(t, BF16) for t in (ca, cb, cc)] + [jnp.asarray(t) for t in (svec, s2vec, vecs)]


T2, BASE, W1, W2, REP = 0, 640, 1280, 2000, 2720


def div(a, n):
    return lax.div(a, jnp.int32(n))


def mod(a, n):
    return lax.rem(a, jnp.int32(n))


def band_of(z, y, half, hemi):
    even = jnp.where(hemi == 0, 2 * half, 6 - 2 * half)
    delta = mod(z - even + 8, 8)
    near = jnp.logical_and(delta >= 1, delta <= 4)
    band = jnp.where(near, even + 1, even) * 8 + y
    quarter = jnp.where(near, delta - 1, mod(8 - delta, 8))
    return band, quarter


def block_of(z, y, half, hemi):
    band, quarter = band_of(z, y, half, hemi)
    return jnp.where(hemi == 0, 4 * (band - 16 * half) + quarter, 4 * (63 - band - 16 * half) + 3 - quarter)


def owner_of(band, quarter, field):
    hemi = div(band, 32)
    north = jnp.where(hemi == 0, band, 63 - band)
    z, y = div(band, 8), mod(band, 8)
    z = mod(z + jnp.where(mod(z, 2) == 1, quarter, 8 - quarter), 8)
    return z * 8 + y, 2 * (4 * div(north, 16) + field) + hemi


def iota(shape, dim):
    return lax.broadcasted_iota(I32, shape, dim)


def dot(x, y):
    return jnp.dot(x, y, preferred_element_type=F32)


def kernel(
    spec, leg_hbm, pairs_s, pairs, limits, forcing_hbm, helm, ca, cb, cc, svec, s2vec, vecs,
    grid_out, spec_out,
    leg, forcing, cav, cbv, ccv, spec_t, mix, fac, mul_t, fpad, fsend, fsend2, rwx, part, prcv, summ, xrcv, xsum,
    xt, tt, smat, s2m, oht, oh, texp, bbuf, brcv, frcv, frcv2, lines, rwrcv, bd, gbuf, gbuf2, grcv, grcv2, abuf, ebuf, ercv, fall,
    csem, psem, fs, fr, xs, xr, bs, br, es, er, gs, gr, as_, ar, ws, wr,
):
    lat, lon = lax.axis_index("lat"), lax.axis_index("lon")
    chip, core = div(lon, 2), mod(lon, 2)
    half, field = div(chip, 4), mod(chip, 4)
    zc, yc = div(lat, 8), mod(lat, 8)
    partner = 2 * chip + 1 - core
    band, quarter = band_of(zc, yc, half, core)

    barrier = pltpu.get_barrier_semaphore()

    def greet(to_lat, to_lon):
        pl.semaphore_signal(barrier, inc=1, device_id=(to_lat, to_lon), device_id_type=MESH)

    def far_first(n):
        return mod(zc + 4 + div(n, 8), 8), mod(yc + 4 + mod(n, 8), 8)

    def others(action):
        @pl.loop(0, 36)
        def _(n):
            action(*far_first(n))

        @pl.loop(37, 64)
        def _(n):
            action(*far_first(n))

    others(lambda to_z, to_y: greet(to_z * 8 + to_y, lon))

    @pl.loop(0, 16)
    def _(n):
        to_lat, to_lon = owner_of(lat, div(n, 4), mod(n, 4))

        @pl.when(jnp.logical_or(to_lat != lat, to_lon != lon))
        def _():
            greet(to_lat, to_lon)

        @pl.when(jnp.logical_or(band != lat, n != lon))
        def _():
            greet(band, n)

    greet(lat, partner)

    @pl.loop(1, 8)
    def _(t):
        greet(lat, 2 * mod(chip + t, 8) + core)

    loads = [
        pltpu.make_async_copy(src, dst, csem.at[n])
        for n, (src, dst) in enumerate(
            [(leg_hbm, leg), (forcing_hbm, forcing), (ca, cav), (cb, cbv), (cc, ccv)]
        )
    ]
    for copy in loads:
        copy.start()

    row, col = iota((64, 84), 0), iota((64, 84), 1) + lon * 84
    second_wave, hemi_row = row % 2 == 1, row // 32 == 1
    pick = (row[:, :8] // 8 % 4 * 2 + row[:, :8] // 2 % 2 == iota((64, 8), 1)).astype(F32)
    low_col = iota((8, 84), 1) + lon * 84
    field_row = iota((8, 84), 0) // 2
    helm_row = jnp.full((8, 84), helm[3])
    for f in range(3):
        helm_row = jnp.where(field_row == f, helm[f], helm_row)

    @pl.loop(0, 10)
    def _(s):
        v = pairs_s[10 * lat + s]
        for f in range(4):
            spec_t[s, 2 * f : 2 * f + 2, :] = spec[f, s]
        edge = M - v
        first = col < edge
        second = jnp.logical_and(col < M + 1, jnp.logical_not(first))
        odd = jnp.where(first, col, col - edge) % 2 == 1
        used = jnp.logical_or(
            jnp.logical_and(second_wave, second), jnp.logical_and(jnp.logical_not(second_wave), first)
        )
        used = jnp.logical_and(used, row // 4 % 2 == s % 2)
        factor = jnp.where(used, jnp.where(jnp.logical_and(hemi_row, odd), -1.0, 1.0), 0.0)
        rounded = spec_t[s].astype(BF16).astype(F32)
        mix[s] = (factor * dot(pick, rounded)).astype(BF16)
        fac[s] = factor * math.sqrt(M)
        degree = jnp.where(low_col < edge, v + low_col, low_col - 1).astype(F32)
        valid = (low_col < M + 1).astype(F32)
        mul_t[s] = valid / (1.0 + helm_row * (degree * (degree + 1.0)))

    loads[0].wait()

    @pl.loop(0, 5)
    def _(sp):
        terms = dot(mix[2 * sp], leg[2 * sp]) + dot(mix[2 * sp + 1], leg[2 * sp + 1])
        terms = (terms * (0.5 / math.sqrt(M))).astype(BF16)
        part[:, :, sp] = terms.reshape(2, 4, 8, M)

    loads[1].wait()
    for f in range(4):
        for w in range(4):
            fpad[f, w, 0:10, :] = forcing[f, 10 * w : 10 * w + 10, :]
    fsend[...] = fpad[:, :, 0:8, :].astype(BF16)
    fsend2[...] = fpad[:, :, 8:10, :].astype(BF16)
    rwx[...] = jnp.zeros_like(rwx)
    rwx[:, 0:40] = jnp.broadcast_to(limits[...].astype(F32), (8, 40))

    my_slot_lat, my_slot_lon = owner_of(lat, 0, field)
    is_self = jnp.logical_and(my_slot_lat == lat, my_slot_lon == lon)
    pl.semaphore_wait(barrier, 103 - 2 * is_self.astype(I32))

    swap = pltpu.make_async_remote_copy(
        part.at[1 - core], prcv, psem.at[0], psem.at[1], device_id=(lat, partner), device_id_type=MESH
    )
    swap.start()

    def forcing_copy(n):
        to_lat, to_lon = owner_of(lat, div(n, 4), mod(n, 4))
        away = jnp.logical_or(to_lat != lat, to_lon != lon)
        pieces = []
        for n2, (src, dst) in enumerate([(fsend, frcv), (fsend2, frcv2)]):
            src, dst = src.at[mod(n, 4), div(n, 4)], dst.at[lon]
            remote = pltpu.make_async_remote_copy(
                src, dst, fs.at[n2, n], fr.at[n2], device_id=(to_lat, to_lon), device_id_type=MESH
            )
            pieces.append((remote, pltpu.make_async_copy(src, dst, fr.at[n2])))
        return away, pieces

    def rows_copy():
        to_lat, to_lon = owner_of(lat, div(lon, 4), mod(lon, 4))
        away = jnp.logical_or(to_lat != lat, to_lon != lon)
        remote = pltpu.make_async_remote_copy(
            rwx, rwrcv, ws, wr, device_id=(to_lat, to_lon), device_id_type=MESH
        )
        return away, [(remote, pltpu.make_async_copy(rwx, rwrcv, wr))]

    def launch(away, pieces):
        @pl.when(away)
        def _():
            for remote, _ in pieces:
                remote.start()

        @pl.when(jnp.logical_not(away))
        def _():
            for _, local in pieces:
                local.start()

    def settle(away, pieces):
        @pl.when(away)
        def _():
            for remote, _ in pieces:
                remote.wait_send()

    @pl.loop(0, 16)
    def _(n):
        launch(*forcing_copy(n))

    launch(*rows_copy())

    swap.wait_recv()
    summ[...] = (part[core].astype(F32) + prcv[...].astype(F32)).astype(BF16)

    step = jnp.where(core == 0, 1, 7)

    def chunk(to):
        return summ.at[mod(to, 4), :, :, pl.ds(pl.multiple_of(640 * div(to, 4), 128), 640)]

    def shared(slot, owner, via, src=None):
        src = chunk(mod(chip + owner * step, 8)) if src is None else src
        to = mod(chip + via * step, 8)
        return pltpu.make_async_remote_copy(
            src, xrcv.at[slot], xs.at[slot], xr.at[slot],
            device_id=(lat, 2 * to + core), device_id_type=MESH,
        )

    opening = [shared(4, 4, 2), shared(3, 3, 1), shared(5, 5, 7), shared(1, 1, 1), shared(7, 7, 7)]
    for copy in opening:
        copy.start()

    lanes = iota((128, 512), 0)
    for i in range(10):
        smat[i] = (svec[core, i : i + 1, :] == lanes).astype(BF16)

    opening[1].wait_recv()
    opening[0].wait_recv()
    onward = chunk(mod(chip + 2 * step, 8))[...].astype(F32) + xrcv[3].astype(F32) + xrcv[4].astype(F32)
    xsum[0] = onward.astype(BF16)
    ahead = shared(2, 2, 2, xsum.at[0])
    ahead.start()
    opening[2].wait_recv()
    onward = chunk(mod(chip + 6 * step, 8))[...].astype(F32) + xrcv[5].astype(F32)
    xsum[1] = onward.astype(BF16)
    behind = shared(6, 6, 6, xsum.at[1])
    behind.start()

    expand = (vecs[0:1, :] == iota((128, M), 0)).astype(BF16)
    loads[2].wait()
    base = cav[BASE : BASE + 640, 0:128]
    texp[...] = dot(base, expand).astype(BF16)
    waves = jnp.concatenate([pairs[t : t + 1, :] for t in range(5)], axis=1)
    waves = jnp.broadcast_to(waves, (16, 640))
    top = iota((16, 640), 0)
    waves = jnp.where(top == 0, waves // 16, jnp.where(top == 1, waves % 16, 0)).astype(F32).astype(BF16)
    where_from = vecs[1:2, 0:768]
    placed = dot(waves, (where_from == iota((640, 768), 0)).astype(BF16))
    place = jnp.where(where_from >= 0, 40.0 * placed[1:2] + placed[0:1], -1.0)
    for s3 in range(3):
        oht[s3] = (place[:, 256 * s3 : 256 * s3 + 256] == iota((640, 256), 0).astype(F32)).astype(BF16)
    for k in range(6):
        across_rows = jnp.broadcast_to(place[:, 128 * k : 128 * k + 128], (128, 128)).T
        for t in range(5):
            oh[128 * k : 128 * k + 128, 128 * t : 128 * t + 128] = (
                across_rows == (iota((128, 128), 1) + 128 * t).astype(F32)
            ).astype(BF16)
    s2m[...] = (s2vec[core, 0:1, :] == iota((512, M), 0)).astype(BF16)

    total = summ[field, :, :, pl.ds(pl.multiple_of(640 * half, 128), 640)].astype(F32)
    opening[3].wait_recv()
    opening[4].wait_recv()
    ahead.wait_recv()
    behind.wait_recv()
    for slot in (1, 7, 2, 6):
        total = total + xrcv[slot].astype(F32)
    xt[0:40, :] = total.reshape(40, 640)
    xt[40:128, :] = jnp.zeros((88, 640), F32)
    tt[...] = xt[...].T
    packed = dot(tt[pl.ds(0, 64, stride=10), :].astype(BF16), smat[0])
    for i in range(1, 10):
        packed += dot(tt[pl.ds(i, 64, stride=10), :].astype(BF16), smat[i])
    for j in range(4):
        bbuf[:, j, :] = packed[:, 128 * j : 128 * j + 128]

    def to_lines(to_z, to_y):
        pltpu.make_async_remote_copy(
            bbuf.at[block_of(to_z, to_y, half, core)], brcv.at[lat], bs, br,
            device_id=(to_z * 8 + to_y, lon), device_id_type=MESH,
        ).start()

    others(to_lines)
    pltpu.make_async_copy(bbuf.at[block_of(zc, yc, half, core)], brcv.at[lat], br).start()
    pltpu.make_async_copy(frcv, frcv, fr.at[0]).wait()
    pltpu.make_async_copy(frcv2, frcv2, fr.at[1]).wait()
    lines[:, 0:8, :] = frcv[...].astype(F32)
    lines[:, 8:10, :] = frcv2[...].astype(F32)
    lines[:, 10:16, :] = jnp.zeros((16, 6, SEG), F32)
    push = lines[...].reshape(256, SEG).T
    pltpu.make_async_copy(rwrcv, rwrcv, wr).wait()
    chosen = (iota((128, 768), 0) == vecs[2:3, 0:768] + 10 * quarter).astype(F32)
    bound = jnp.dot(rwrcv[...], chosen, preferred_element_type=F32, precision=lax.Precision.HIGHEST)
    loads[3].wait()
    loads[4].wait()
    pltpu.make_async_copy(brcv, brcv, br).wait()

    rows = jnp.concatenate([brcv[:, j, :].astype(BF16) for j in range(4)], axis=0)
    coef = jnp.zeros((640, 240), F32)
    for s3 in range(3):
        spread = dot(rows, cav[REP + 128 * s3 : REP + 128 * s3 + 128, :240]).astype(BF16)
        coef += dot(oht[s3], spread)
    lane = iota((40, 240), 1)
    for b in range(16):
        m = iota((40, 240), 0) * 16 + b
        m = jnp.where(lane % 2 == 1, M - 1 - m, m)
        low = 40 * (b % 6)
        keep = jnp.logical_and(lane >= low, lane < low + 40)
        keep = jnp.logical_and(keep, m.astype(F32) < bound[0:1, 0:240])
        value = jnp.where(keep, coef[40 * b : 40 * b + 40], 0.0)
        if b == 0:
            value = jnp.where(m == 0, 0.5 * value, value)
        bd[40 * b : 40 * b + 40, :] = value.astype(BF16)

    sign = jnp.where(iota((1, 240), 1) % 2 == 1, -1.0, 1.0)
    y = jnp.zeros((SEG, 256), F32)
    for g, depth in enumerate((240, 240, 160)):
        cs = dot(cav[T2 : T2 + 640, :depth], bd[240 * g : 240 * g + depth, :])
        c, s = cs[:SEG], cs[SEG:] * sign
        ta = texp[0:SEG, 256 * g : 256 * g + 240].astype(F32)
        tb = texp[SEG:640, 256 * g : 256 * g + 240].astype(F32)
        y += dot((ta * c - tb * s).astype(BF16), cav[W1 + 240 * g : W1 + 240 * g + 240, :])
        y += dot((tb * c + ta * s).astype(BF16), cav[W2 + 240 * g : W2 + 240 * g + 240, :])
    tend = (push - 0.5 * y * y).astype(BF16)
    lines[...] = y.T.reshape(16, 16, SEG)
    gbuf[...] = lines[:, 0:8, :].astype(BF16)
    gbuf2[...] = lines[:, 8:10, :].astype(BF16)

    gc, gi = dot(tend, cbv[0:256, :]), dot(tend, cbv[256:512, :])
    ta, tb = texp[0:SEG, 768:M].astype(F32), texp[SEG:640, 768:M].astype(F32)
    kc = dot(ccv[...], (ta * gc + tb * gi).astype(BF16))
    ks = dot(ccv[...], (ta * gi - tb * gc).astype(BF16))
    lane = iota((40, 512), 1)
    sign = jnp.where(lane % 2 == 1, -1.0, 1.0)
    m = iota((40, 512), 0) * 16 + lane // 32
    m = jnp.where(lane % 2 == 1, M - 1 - m, m)
    scale = jnp.where(m.astype(F32) < bound[0:1, 256:768], 1.0 / NLON, 0.0)
    real = (kc[:40] + sign * ks[40:]) * scale
    imag = (ks[:40] - sign * kc[40:]) * scale
    lane = iota((40, 128), 1)
    for b in range(16):
        tile, off = 128 * (b // 4), 32 * (b % 4)
        re, im = real[:, tile : tile + 128], imag[:, tile : tile + 128]
        re = pltpu.roll(re, (128 - off) % 128, 1) if off else re
        im = pltpu.roll(im, (148 - off) % 128, 1)
        value = jnp.where(lane < 20, re, jnp.where(lane < 40, im, 0.0))
        abuf[0, 40 * b : 40 * b + 40, :] = value.astype(BF16)
        abuf[1, 40 * b : 40 * b + 40, :] = pltpu.roll(value, 40, 1).astype(BF16)
        abuf[2, 40 * b : 40 * b + 40, :] = pltpu.roll(value, 80, 1).astype(BF16)
    back = jnp.zeros((256, 128), F32)
    for s3 in range(3):
        back += dot(oh[256 * s3 : 256 * s3 + 256, :], abuf[s3])
    for j in range(4):
        ebuf[:, j, :] = back[64 * j : 64 * j + 64]

    block = block_of(zc, yc, half, core)

    def to_waves(to_z, to_y):
        to = to_z * 8 + to_y
        pltpu.make_async_remote_copy(
            ebuf.at[to], ercv.at[block], es, er, device_id=(to, lon), device_id_type=MESH
        ).start()

    others(to_waves)
    pltpu.make_async_copy(ebuf.at[lat], ercv.at[block], er).start()

    def grid_copy(n):
        away = jnp.logical_or(band != lat, n != lon)
        pieces = []
        for n2, (src, dst) in enumerate([(gbuf, grcv), (gbuf2, grcv2)]):
            src, dst = src.at[n], dst.at[field, quarter]
            remote = pltpu.make_async_remote_copy(
                src, dst, gs.at[n2, n], gr.at[n2], device_id=(band, n), device_id_type=MESH
            )
            pieces.append((remote, pltpu.make_async_copy(src, dst, gr.at[n2])))
        return away, pieces

    @pl.loop(0, 16)
    def _(n):
        launch(*grid_copy(n))

    pltpu.make_async_copy(ercv, ercv, er).wait()
    rows = jnp.concatenate([ercv[:, j, :].astype(BF16) for j in range(4)], axis=1)
    placed = dot(rows, s2m[...])
    for i in range(10):
        tt[pl.ds(i, 64, stride=10), :] = placed[:, 128 * i : 128 * i + 128]
    xt[...] = tt[...].T
    fall[core, chip] = xt[0:40, :].astype(BF16).reshape(5, 8, 640)

    def held(k):
        return fall.at[core, mod(chip + 64 - k * step, 8)]

    def around(k, have):
        to = mod(chip + (k - have + 8) * step, 8)
        return pltpu.make_async_remote_copy(
            held(have), held(have), as_.at[k], ar.at[k], device_id=(lat, 2 * to + core), device_id_type=MESH
        )

    def across(k):
        return pltpu.make_async_remote_copy(
            held(k), held(k), as_.at[8 + k], ar.at[8 + k], device_id=(lat, partner), device_id_type=MESH
        )

    hops = {2: 0, 6: 0, 1: 0, 7: 0, 4: 2, 3: 2, 5: 6}

    def arrived(k):
        pltpu.make_async_copy(held(k), held(k), ar.at[k]).wait()

    for k in (2, 6, 1, 7):
        around(k, 0).start()
    across(0).start()
    arrived(2)
    around(4, 2).start()
    around(3, 2).start()
    across(2).start()
    arrived(6)
    around(5, 6).start()
    across(6).start()
    for k in (1, 7, 3, 5, 4):
        arrived(k)
        across(k).start()
    for k in range(8):
        pltpu.make_async_copy(held(k), held(k), ar.at[8 + k]).wait()

    nt = (((1,), (1,)), ((), ()))
    of_row = iota((8, 64), 1)
    fold = (of_row // 8 % 4 * 2 + of_row // 2 % 2 == iota((8, 64), 0)).astype(F32)

    @pl.loop(0, 5)
    def _(sp):
        lows, highs = fall[:, 0:4, sp], fall[:, 4:8, sp]
        low = lows.astype(F32).reshape(64, 640).astype(BF16)
        high = highs.astype(F32).reshape(64, 640).astype(BF16)
        for s2 in range(2):
            basis = leg[2 * sp + s2]
            sums = lax.dot_general(low, basis[:, :640], nt, preferred_element_type=F32)
            sums += lax.dot_general(high, basis[:, 640:], nt, preferred_element_type=F32)
            sums = sums * fac[2 * sp + s2]
            folded = jnp.dot(fold, sums, preferred_element_type=F32, precision=lax.Precision.HIGHEST)
            done = (spec_t[2 * sp + s2] + folded) * mul_t[2 * sp + s2]
            for f in range(4):
                spec_out[f, 2 * sp + s2] = done[2 * f : 2 * f + 2]

    pltpu.make_async_copy(grcv, grcv, gr.at[0]).wait()
    pltpu.make_async_copy(grcv2, grcv2, gr.at[1]).wait()
    for f in range(4):
        for w in range(4):
            grid_out[f, 10 * w : 10 * w + 8, :] = grcv[f, w].astype(F32)
            grid_out[f, 10 * w + 8 : 10 * w + 10, :] = grcv2[f, w].astype(F32)

    swap.wait_send()
    for copy in opening + [ahead, behind]:
        copy.wait_send()
    for k, have in hops.items():
        around(k, have).wait_send()
    for k in range(8):
        across(k).wait_send()
    rest = brcv.at[pl.ds(0, 63)]
    pltpu.make_async_copy(rest, rest, bs).wait()
    pltpu.make_async_copy(rest, rest, es).wait()

    @pl.loop(0, 16)
    def _(n):
        settle(*forcing_copy(n))
        settle(*grid_copy(n))

    settle(*rows_copy())


def body(spec, legendre, wave_pairs, row_waves, forcing, helm_coef):
    vmem, hbm = pl.BlockSpec(memory_space=pltpu.VMEM), pl.BlockSpec(memory_space=pl.ANY)
    smem = pl.BlockSpec(memory_space=pltpu.SMEM)
    dma = pltpu.SemaphoreType.DMA

    def v16(*shape):
        return pltpu.VMEM(shape, BF16)

    def v32(*shape):
        return pltpu.VMEM(shape, F32)

    grid_field, spec_new = pl.pallas_call(
        kernel,
        out_shape=(
            v32(4, 40, SEG),
            v32(4, 10, 2, 84),
        ),
        in_specs=[vmem, hbm, smem, vmem, vmem, hbm, smem, hbm, hbm, hbm, vmem, vmem, vmem],
        out_specs=(vmem, vmem),
        scratch_shapes=[
            v16(10, 84, M), v32(4, 40, SEG), v16(3104, 256), v16(512, 512), v16(80, SEG), v32(10, 8, 84),
            v16(10, 64, 84), v32(10, 64, 84), v32(10, 8, 84), v32(4, 4, 16, SEG), v16(4, 4, 8, SEG), v16(4, 4, 2, SEG), v32(8, 128),
            v16(2, 4, 5, 8, M), v16(4, 5, 8, M), v16(4, 5, 8, M), v16(8, 5, 8, 640), v16(2, 5, 8, 640),
            v32(128, 640), v32(640, 128), v16(10, 128, 512), v16(512, M), v16(3, 640, 256), v16(768, 640),
            v16(640, M), v32(64, 4, 128), v32(64, 4, 128), v16(16, 8, SEG), v16(16, 2, SEG), v32(16, 16, SEG), v32(8, 128),
            v16(640, 240), v16(16, 8, SEG), v16(16, 2, SEG), v16(4, 4, 8, SEG), v16(4, 4, 2, SEG), v16(3, 640, 128), v32(64, 4, 128),
            v32(64, 4, 128), v16(2, 8, 5, 8, 640),
            dma((5,)), dma((2,)), dma((2, 16)), dma((2,)), dma((8,)), dma((8,)), dma, dma, dma, dma,
            dma((2, 16)), dma((2,)), dma((16,)), dma((16,)), dma, dma,
        ],
        compiler_params=pltpu.CompilerParams(
            collective_id=0, has_side_effects=True, vmem_limit_bytes=60 * 1024 * 1024
        ),
        name="step",
    )(
        jnp.transpose(spec, (0, 2, 1, 3)), legendre, wave_pairs, wave_pairs.reshape(5, 128),
        row_waves.reshape(1, 40), forcing, helm_coef, *tables(),
    )
    return (grid_field, jnp.transpose(spec_new, (0, 2, 1, 3)))


def solution(mesh):
    return jax.shard_map(
        body,
        mesh=mesh,
        in_specs=(
            P(None, None, "lat", "lon"),
            P("lat", "lon", None),
            P(),
            P("lat"),
            P(None, "lat", "lon"),
            P(),
        ),
        out_specs=(P(None, "lat", "lon"), P(None, None, "lat", "lon")),
        check_vma=False,
    )
```

```python
import math

import jax
import jax.numpy as jnp
import numpy as np
from jax import lax
from jax.experimental import pallas as pl
from jax.experimental.pallas import tpu as pltpu
from jax.sharding import PartitionSpec as P

M = 1280
NLON = 5120
SEG = 320
MESH = pl.DeviceIdType.MESH
F32, BF16, I32 = jnp.float32, jnp.bfloat16, jnp.int32


def tables():
    x = np.arange(SEG)
    a = np.arange(40)
    psi = 2 * np.pi * ((a[None, :] * x[:, None]) % SEG) / SEG
    cos_ax, sin_ax = np.cos(psi), np.sin(psi)

    def alpha(b, q):
        m = np.where(q == 0, b, M - 1 - b)
        return 2 * np.pi * ((m[None, :] * x[:, None]) % NLON) / NLON

    t2rep = np.zeros((640, 256))
    t2rep[:, :240] = np.tile(np.concatenate([cos_ax, sin_ax]), (1, 6))
    base = np.zeros((640, 256))
    slot = np.arange(32)
    base[:, :32] = np.concatenate([np.cos(alpha(slot // 2, slot % 2)), np.sin(alpha(slot // 2, slot % 2))])
    lane = np.arange(240)
    b6, r, i, q = lane // 40, lane % 40 // 20, lane % 20 // 2, lane % 2
    w1, w2 = np.zeros((3, 240, 256)), np.zeros((3, 240, 256))
    col = np.arange(256)
    d, icol = col // 16, col % 16
    vecs = np.full((8, M), -1, np.int32)
    for g in range(3):
        b = 6 * g + b6
        ok = b < 16
        vecs[0, 256 * g : 256 * g + 240] = np.where(ok, 2 * b + q, -1)
        bq = np.where(q == 0, b, 15 - b)
        beta = 2 * np.pi * ((bq[:, None] * d[None, :]) % 16) / 16
        same = (i[:, None] == icol[None, :]) * ok[:, None] * 2.0
        w1[g] = same * np.where(r[:, None] == 0, np.cos(beta), -np.sin(beta))
        w2[g] = same * np.where(r[:, None] == 0, -np.sin(beta), -np.cos(beta))
    rep = np.zeros((3, 128, 256))
    for s3 in range(3):
        rep[s3, 40 * s3 + lane % 40, lane] = 1.0
    ca = np.concatenate([t2rep, base, *w1, *w2, *rep])
    vecs[2, :240] = i
    vecs[2, 240:768] = -1000
    lane = np.arange(512)
    b, i, q = lane // 32, lane % 32 // 2, lane % 2
    ok = lane % 32 < 20
    vecs[0, 768:] = np.where(ok, 2 * b + q, -1)
    vecs[2, 256:768] = np.where(ok, i, -1000)
    bq = np.where(q == 0, b, 15 - b)
    beta = 2 * np.pi * ((bq[None, :] * d[:, None]) % 16) / 16
    same = (i[None, :] == icol[:, None]) * ok[None, :] * 1.0
    cb = np.concatenate([same * np.cos(beta), -same * np.sin(beta)])
    cc = np.concatenate([cos_ax.T, sin_ax.T])
    lane = np.arange(768)
    s = 3 * (lane % 256 // 64) + lane // 256
    vecs[1, :768] = np.where(s < 10, 10 * (lane % 64) + s, -1)
    svec = np.full((2, 16, 512), -1, np.int32)
    s2vec = np.full((2, 8, M), -1, np.int32)
    for core in range(2):
        for i in range(10):
            line = i if core == 0 else 9 - i
            for rho in range(40):
                s, r, q = rho // 4, rho % 4 // 2, rho % 2
                target = s // 3 * 128 + s % 3 * 40 + r * 20 + line * 2 + q
                svec[core, i, target] = rho
                s2vec[core, :, i * 128 + rho] = target
    return [jnp.asarray(t, BF16) for t in (ca, cb, cc)] + [jnp.asarray(t) for t in (svec, s2vec, vecs)]


T2, BASE, W1, W2, REP = 0, 640, 1280, 2000, 2720


def div(a, n):
    return lax.div(a, jnp.int32(n))


def mod(a, n):
    return lax.rem(a, jnp.int32(n))


def band_of(z, y, half, hemi):
    even = jnp.where(hemi == 0, 2 * half, 6 - 2 * half)
    delta = mod(z - even + 8, 8)
    near = jnp.logical_and(delta >= 1, delta <= 4)
    band = jnp.where(near, even + 1, even) * 8 + y
    quarter = jnp.where(near, delta - 1, mod(8 - delta, 8))
    return band, quarter


def block_of(z, y, half, hemi):
    band, quarter = band_of(z, y, half, hemi)
    return jnp.where(hemi == 0, 4 * (band - 16 * half) + quarter, 4 * (63 - band - 16 * half) + 3 - quarter)


def owner_of(band, quarter, field):
    hemi = div(band, 32)
    north = jnp.where(hemi == 0, band, 63 - band)
    z, y = div(band, 8), mod(band, 8)
    z = mod(z + jnp.where(mod(z, 2) == 1, quarter, 8 - quarter), 8)
    return z * 8 + y, 2 * (4 * div(north, 16) + field) + hemi


def iota(shape, dim):
    return lax.broadcasted_iota(I32, shape, dim)


def dot(x, y):
    return jnp.dot(x, y, preferred_element_type=F32)


def kernel(
    leg_hbm, forcing_hbm, ca, cb, cc, spec_hbm, pairs_hbm, limits_hbm, helm_hbm, svec_hbm, s2vec_hbm, vecs_hbm,
    grid_out, spec_out,
    leg, forcing, cav, cbv, ccv, spec, pairs, limits, helm, svec, s2vec, vecs, vcol, spec_t, mix, fac, mul_t, fpad, fsend, fsend2, rwx, part, prcv, summ, xrcv, xsum,
    xt, tt, smat, s2m, oht, oh, texp, bbuf, brcv, frcv, frcv2, lines, rwrcv, bd, gbuf, gbuf2, grcv, grcv2, abuf, ebuf, ercv, fall,
    csem, psem, fs, fr, xs, xr, bs, br, es, er, gs, gr, as_, ar, ws, wr,
):
    lat, lon = lax.axis_index("lat"), lax.axis_index("lon")
    chip, core = div(lon, 2), mod(lon, 2)
    half, field = div(chip, 4), mod(chip, 4)
    zc, yc = div(lat, 8), mod(lat, 8)
    partner = 2 * chip + 1 - core
    band, quarter = band_of(zc, yc, half, core)

    barrier = pltpu.get_barrier_semaphore()

    def greet(to_lat, to_lon):
        pl.semaphore_signal(barrier, inc=1, device_id=(to_lat, to_lon), device_id_type=MESH)

    def far_first(n):
        return mod(zc + 4 + div(n, 8), 8), mod(yc + 4 + mod(n, 8), 8)

    def others(action):
        @pl.loop(0, 36)
        def _(n):
            action(*far_first(n))

        @pl.loop(37, 64)
        def _(n):
            action(*far_first(n))

    others(lambda to_z, to_y: greet(to_z * 8 + to_y, lon))

    @pl.loop(0, 16)
    def _(n):
        to_lat, to_lon = owner_of(lat, div(n, 4), mod(n, 4))

        @pl.when(jnp.logical_or(to_lat != lat, to_lon != lon))
        def _():
            greet(to_lat, to_lon)

        @pl.when(jnp.logical_or(band != lat, n != lon))
        def _():
            greet(band, n)

    greet(lat, partner)

    @pl.loop(1, 8)
    def _(t):
        greet(lat, 2 * mod(chip + t, 8) + core)

    loads = [
        pltpu.make_async_copy(src, dst, csem.at[n])
        for n, (src, dst) in enumerate(
            [
                (leg_hbm, leg), (forcing_hbm, forcing), (ca, cav), (cb, cbv), (cc, ccv), (spec_hbm, spec),
                (pairs_hbm, pairs), (limits_hbm, limits), (helm_hbm, helm), (svec_hbm, svec),
                (s2vec_hbm, s2vec), (vecs_hbm, vecs),
            ]
        )
    ]
    for n in (6, 5, 8, 0, 1, 7, 9, 11, 10, 2, 3, 4):
        loads[n].start()

    row, col = iota((64, 84), 0), iota((64, 84), 1) + lon * 84
    second_wave, hemi_row = row % 2 == 1, row // 32 == 1
    pick = (row[:, :8] // 8 % 4 * 2 + row[:, :8] // 2 % 2 == iota((64, 8), 1)).astype(F32)
    low_col = iota((8, 84), 1) + lon * 84
    field_row = iota((8, 84), 0) // 2
    loads[8].wait()
    helm_row = jnp.broadcast_to(helm[0:1, 3:4], (8, 84))
    for f in range(3):
        helm_row = jnp.where(field_row == f, jnp.broadcast_to(helm[0:1, f : f + 1], (8, 84)), helm_row)
    loads[6].wait()
    waves = jnp.concatenate([pairs[t : t + 1, :] for t in range(5)], axis=1)
    ours = iota((16, 640), 1) == iota((16, 640), 0) + 10 * lat
    ours = jnp.sum(jnp.where(ours, jnp.broadcast_to(waves, (16, 640)).astype(F32), 0.0), axis=1, keepdims=True)
    vcol[...] = jnp.broadcast_to(ours, (16, 128))
    loads[5].wait()

    @pl.loop(0, 10)
    def _(s):
        v = vcol[pl.ds(s, 1), 0:84].astype(I32)
        for f in range(4):
            spec_t[s, 2 * f : 2 * f + 2, :] = spec[f, s]
        edge = M - v
        first = col < edge
        second = jnp.logical_and(col < M + 1, jnp.logical_not(first))
        odd = jnp.where(first, col, col - edge) % 2 == 1
        used = jnp.logical_or(
            jnp.logical_and(second_wave, second), jnp.logical_and(jnp.logical_not(second_wave), first)
        )
        used = jnp.logical_and(used, row // 4 % 2 == s % 2)
        factor = jnp.where(used, jnp.where(jnp.logical_and(hemi_row, odd), -1.0, 1.0), 0.0)
        rounded = spec_t[s].astype(BF16).astype(F32)
        mix[s] = (factor * dot(pick, rounded)).astype(BF16)
        fac[s] = factor * math.sqrt(M)
        degree = jnp.where(low_col < edge, v + low_col, low_col - 1).astype(F32)
        valid = (low_col < M + 1).astype(F32)
        mul_t[s] = valid / (1.0 + helm_row * (degree * (degree + 1.0)))

    loads[0].wait()

    @pl.loop(0, 5)
    def _(sp):
        terms = dot(mix[2 * sp], leg[2 * sp]) + dot(mix[2 * sp + 1], leg[2 * sp + 1])
        terms = (terms * (0.5 / math.sqrt(M))).astype(BF16)
        part[:, :, sp] = terms.reshape(2, 4, 8, M)

    loads[1].wait()
    for f in range(4):
        for w in range(4):
            fpad[f, w, 0:10, :] = forcing[f, 10 * w : 10 * w + 10, :]
    fsend[...] = fpad[:, :, 0:8, :].astype(BF16)
    fsend2[...] = fpad[:, :, 8:10, :].astype(BF16)
    loads[7].wait()
    rwx[...] = jnp.zeros_like(rwx)
    rwx[:, 0:40] = jnp.broadcast_to(limits[...].astype(F32), (8, 40))

    my_slot_lat, my_slot_lon = owner_of(lat, 0, field)
    is_self = jnp.logical_and(my_slot_lat == lat, my_slot_lon == lon)
    pl.semaphore_wait(barrier, 103 - 2 * is_self.astype(I32))

    step = jnp.where(core == 0, 1, 7)

    def swap(n, toward):
        f = mod(chip + (0, 3, 1, 2)[n] * toward, 4)
        return pltpu.make_async_remote_copy(
            part.at[1 - core, f], prcv.at[f], psem.at[0, n], psem.at[1, n],
            device_id=(lat, partner), device_id_type=MESH,
        )

    for n in range(4):
        swap(n, 8 - step).start()

    def forcing_copy(n):
        to_lat, to_lon = owner_of(lat, div(n, 4), mod(n, 4))
        away = jnp.logical_or(to_lat != lat, to_lon != lon)
        pieces = []
        for n2, (src, dst) in enumerate([(fsend, frcv), (fsend2, frcv2)]):
            src, dst = src.at[mod(n, 4), div(n, 4)], dst.at[lon]
            remote = pltpu.make_async_remote_copy(
                src, dst, fs.at[n2, n], fr.at[n2], device_id=(to_lat, to_lon), device_id_type=MESH
            )
            pieces.append((remote, pltpu.make_async_copy(src, dst, fr.at[n2])))
        return away, pieces

    def rows_copy():
        to_lat, to_lon = owner_of(lat, div(lon, 4), mod(lon, 4))
        away = jnp.logical_or(to_lat != lat, to_lon != lon)
        remote = pltpu.make_async_remote_copy(
            rwx, rwrcv, ws, wr, device_id=(to_lat, to_lon), device_id_type=MESH
        )
        return away, [(remote, pltpu.make_async_copy(rwx, rwrcv, wr))]

    def launch(away, pieces):
        @pl.when(away)
        def _():
            for remote, _ in pieces:
                remote.start()

        @pl.when(jnp.logical_not(away))
        def _():
            for _, local in pieces:
                local.start()

    def settle(away, pieces):
        @pl.when(away)
        def _():
            for remote, _ in pieces:
                remote.wait_send()

    @pl.loop(0, 16)
    def _(n):
        launch(*forcing_copy(n))

    launch(*rows_copy())

    def chunk(to):
        return summ.at[mod(to, 4), :, :, pl.ds(pl.multiple_of(640 * div(to, 4), 128), 640)]

    def shared(slot, owner, via, src=None):
        src = chunk(mod(chip + owner * step, 8)) if src is None else src
        to = mod(chip + via * step, 8)
        return pltpu.make_async_remote_copy(
            src, xrcv.at[slot], xs.at[slot], xr.at[slot],
            device_id=(lat, 2 * to + core), device_id_type=MESH,
        )

    opening = [shared(4, 4, 2), shared(3, 3, 1), shared(5, 5, 7), shared(1, 1, 1), shared(7, 7, 7)]
    for n, ready in enumerate(((0,), (1, 4), (2, 3), ())):
        swap(n, step).wait_recv()
        f = mod(chip + (0, 3, 1, 2)[n] * step, 4)
        summ[f] = (part[core, f].astype(F32) + prcv[f].astype(F32)).astype(BF16)
        for k in ready:
            opening[k].start()

    for n in (9, 10, 11):
        loads[n].wait()
    lanes = iota((128, 512), 0)
    for i in range(10):
        smat[i] = (svec[core, i : i + 1, :] == lanes).astype(BF16)

    opening[1].wait_recv()
    opening[0].wait_recv()
    onward = chunk(mod(chip + 2 * step, 8))[...].astype(F32) + xrcv[3].astype(F32) + xrcv[4].astype(F32)
    xsum[0] = onward.astype(BF16)
    ahead = shared(2, 2, 2, xsum.at[0])
    ahead.start()
    opening[2].wait_recv()
    onward = chunk(mod(chip + 6 * step, 8))[...].astype(F32) + xrcv[5].astype(F32)
    xsum[1] = onward.astype(BF16)
    behind = shared(6, 6, 6, xsum.at[1])
    behind.start()

    expand = (vecs[0:1, :] == iota((128, M), 0)).astype(BF16)
    loads[2].wait()
    base = cav[BASE : BASE + 640, 0:128]
    texp[...] = dot(base, expand).astype(BF16)
    waves = jnp.broadcast_to(waves, (16, 640))
    top = iota((16, 640), 0)
    waves = jnp.where(top == 0, waves // 16, jnp.where(top == 1, waves % 16, 0)).astype(F32).astype(BF16)
    where_from = vecs[1:2, 0:768]
    placed = dot(waves, (where_from == iota((640, 768), 0)).astype(BF16))
    place = jnp.where(where_from >= 0, 40.0 * placed[1:2] + placed[0:1], -1.0)
    for s3 in range(3):
        oht[s3] = (place[:, 256 * s3 : 256 * s3 + 256] == iota((640, 256), 0).astype(F32)).astype(BF16)
    for k in range(6):
        across_rows = jnp.broadcast_to(place[:, 128 * k : 128 * k + 128], (128, 128)).T
        for t in range(5):
            oh[128 * k : 128 * k + 128, 128 * t : 128 * t + 128] = (
                across_rows == (iota((128, 128), 1) + 128 * t).astype(F32)
            ).astype(BF16)
    s2m[...] = (s2vec[core, 0:1, :] == iota((512, M), 0)).astype(BF16)

    total = summ[field, :, :, pl.ds(pl.multiple_of(640 * half, 128), 640)].astype(F32)
    opening[3].wait_recv()
    opening[4].wait_recv()
    ahead.wait_recv()
    behind.wait_recv()
    for slot in (1, 7, 2, 6):
        total = total + xrcv[slot].astype(F32)
    xt[0:40, :] = total.reshape(40, 640)
    xt[40:128, :] = jnp.zeros((88, 640), F32)
    tt[...] = xt[...].T
    packed = dot(tt[pl.ds(0, 64, stride=10), :].astype(BF16), smat[0])
    for i in range(1, 10):
        packed += dot(tt[pl.ds(i, 64, stride=10), :].astype(BF16), smat[i])
    for j in range(4):
        bbuf[:, j, :] = packed[:, 128 * j : 128 * j + 128]

    def to_lines(to_z, to_y):
        pltpu.make_async_remote_copy(
            bbuf.at[block_of(to_z, to_y, half, core)], brcv.at[lat], bs, br,
            device_id=(to_z * 8 + to_y, lon), device_id_type=MESH,
        ).start()

    others(to_lines)
    pltpu.make_async_copy(bbuf.at[block_of(zc, yc, half, core)], brcv.at[lat], br).start()
    pltpu.make_async_copy(frcv, frcv, fr.at[0]).wait()
    pltpu.make_async_copy(frcv2, frcv2, fr.at[1]).wait()
    lines[:, 0:8, :] = frcv[...].astype(F32)
    lines[:, 8:10, :] = frcv2[...].astype(F32)
    lines[:, 10:16, :] = jnp.zeros((16, 6, SEG), F32)
    push = lines[...].reshape(256, SEG).T
    pltpu.make_async_copy(rwrcv, rwrcv, wr).wait()
    chosen = (iota((128, 768), 0) == vecs[2:3, 0:768] + 10 * quarter).astype(F32)
    bound = jnp.dot(rwrcv[...], chosen, preferred_element_type=F32, precision=lax.Precision.HIGHEST)
    loads[3].wait()
    loads[4].wait()
    pltpu.make_async_copy(brcv, brcv, br).wait()

    rows = jnp.concatenate([brcv[:, j, :].astype(BF16) for j in range(4)], axis=0)
    coef = jnp.zeros((640, 240), F32)
    for s3 in range(3):
        spread = dot(rows, cav[REP + 128 * s3 : REP + 128 * s3 + 128, :240]).astype(BF16)
        coef += dot(oht[s3], spread)
    lane = iota((40, 240), 1)
    for b in range(16):
        m = iota((40, 240), 0) * 16 + b
        m = jnp.where(lane % 2 == 1, M - 1 - m, m)
        low = 40 * (b % 6)
        keep = jnp.logical_and(lane >= low, lane < low + 40)
        keep = jnp.logical_and(keep, m.astype(F32) < bound[0:1, 0:240])
        value = jnp.where(keep, coef[40 * b : 40 * b + 40], 0.0)
        if b == 0:
            value = jnp.where(m == 0, 0.5 * value, value)
        bd[40 * b : 40 * b + 40, :] = value.astype(BF16)

    sign = jnp.where(iota((1, 240), 1) % 2 == 1, -1.0, 1.0)
    y = jnp.zeros((SEG, 256), F32)
    for g, depth in enumerate((240, 240, 160)):
        cs = dot(cav[T2 : T2 + 640, :depth], bd[240 * g : 240 * g + depth, :])
        c, s = cs[:SEG], cs[SEG:] * sign
        ta = texp[0:SEG, 256 * g : 256 * g + 240].astype(F32)
        tb = texp[SEG:640, 256 * g : 256 * g + 240].astype(F32)
        y += dot((ta * c - tb * s).astype(BF16), cav[W1 + 240 * g : W1 + 240 * g + 240, :])
        y += dot((tb * c + ta * s).astype(BF16), cav[W2 + 240 * g : W2 + 240 * g + 240, :])
    tend = (push - 0.5 * y * y).astype(BF16)
    lines[...] = y.T.reshape(16, 16, SEG)
    gbuf[...] = lines[:, 0:8, :].astype(BF16)
    gbuf2[...] = lines[:, 8:10, :].astype(BF16)

    gc, gi = dot(tend, cbv[0:256, :]), dot(tend, cbv[256:512, :])
    ta, tb = texp[0:SEG, 768:M].astype(F32), texp[SEG:640, 768:M].astype(F32)
    kc = dot(ccv[...], (ta * gc + tb * gi).astype(BF16))
    ks = dot(ccv[...], (ta * gi - tb * gc).astype(BF16))
    lane = iota((40, 512), 1)
    sign = jnp.where(lane % 2 == 1, -1.0, 1.0)
    m = iota((40, 512), 0) * 16 + lane // 32
    m = jnp.where(lane % 2 == 1, M - 1 - m, m)
    scale = jnp.where(m.astype(F32) < bound[0:1, 256:768], 1.0 / NLON, 0.0)
    real = (kc[:40] + sign * ks[40:]) * scale
    imag = (ks[:40] - sign * kc[40:]) * scale
    lane = iota((40, 128), 1)
    for b in range(16):
        tile, off = 128 * (b // 4), 32 * (b % 4)
        re, im = real[:, tile : tile + 128], imag[:, tile : tile + 128]
        re = pltpu.roll(re, (128 - off) % 128, 1) if off else re
        im = pltpu.roll(im, (148 - off) % 128, 1)
        value = jnp.where(lane < 20, re, jnp.where(lane < 40, im, 0.0))
        abuf[0, 40 * b : 40 * b + 40, :] = value.astype(BF16)
        abuf[1, 40 * b : 40 * b + 40, :] = pltpu.roll(value, 40, 1).astype(BF16)
        abuf[2, 40 * b : 40 * b + 40, :] = pltpu.roll(value, 80, 1).astype(BF16)
    back = jnp.zeros((256, 128), F32)
    for s3 in range(3):
        back += dot(oh[256 * s3 : 256 * s3 + 256, :], abuf[s3])
    for j in range(4):
        ebuf[:, j, :] = back[64 * j : 64 * j + 64]

    block = block_of(zc, yc, half, core)

    def to_waves(to_z, to_y):
        to = to_z * 8 + to_y
        pltpu.make_async_remote_copy(
            ebuf.at[to], ercv.at[block], es, er, device_id=(to, lon), device_id_type=MESH
        ).start()

    others(to_waves)
    pltpu.make_async_copy(ebuf.at[lat], ercv.at[block], er).start()

    def grid_copy(n):
        away = jnp.logical_or(band != lat, n != lon)
        pieces = []
        for n2, (src, dst) in enumerate([(gbuf, grcv), (gbuf2, grcv2)]):
            src, dst = src.at[n], dst.at[field, quarter]
            remote = pltpu.make_async_remote_copy(
                src, dst, gs.at[n2, n], gr.at[n2], device_id=(band, n), device_id_type=MESH
            )
            pieces.append((remote, pltpu.make_async_copy(src, dst, gr.at[n2])))
        return away, pieces

    @pl.loop(0, 16)
    def _(n):
        launch(*grid_copy(n))

    pltpu.make_async_copy(ercv, ercv, er).wait()
    rows = jnp.concatenate([ercv[:, j, :].astype(BF16) for j in range(4)], axis=1)
    placed = dot(rows, s2m[...])
    for i in range(10):
        tt[pl.ds(i, 64, stride=10), :] = placed[:, 128 * i : 128 * i + 128]
    xt[...] = tt[...].T
    fall[core, chip] = xt[0:40, :].astype(BF16).reshape(5, 8, 640)

    def held(k):
        return fall.at[core, mod(chip + 64 - k * step, 8)]

    def around(k, have):
        to = mod(chip + (k - have + 8) * step, 8)
        return pltpu.make_async_remote_copy(
            held(have), held(have), as_.at[k], ar.at[k], device_id=(lat, 2 * to + core), device_id_type=MESH
        )

    def across(k):
        return pltpu.make_async_remote_copy(
            held(k), held(k), as_.at[8 + k], ar.at[8 + k], device_id=(lat, partner), device_id_type=MESH
        )

    hops = {2: 0, 6: 0, 1: 0, 7: 0, 4: 2, 3: 2, 5: 6}

    def arrived(k):
        pltpu.make_async_copy(held(k), held(k), ar.at[k]).wait()

    for k in (2, 6, 1, 7):
        around(k, 0).start()
    across(0).start()
    arrived(2)
    around(4, 2).start()
    around(3, 2).start()
    across(2).start()
    arrived(6)
    around(5, 6).start()
    across(6).start()
    for k in (1, 7, 3, 5, 4):
        arrived(k)
        across(k).start()
    pltpu.make_async_copy(grcv, grcv, gr.at[0]).wait()
    pltpu.make_async_copy(grcv2, grcv2, gr.at[1]).wait()
    for f in range(4):
        for w in range(4):
            grid_out[f, 10 * w : 10 * w + 8, :] = grcv[f, w].astype(F32)
            grid_out[f, 10 * w + 8 : 10 * w + 10, :] = grcv2[f, w].astype(F32)

    for k in range(8):
        pltpu.make_async_copy(held(k), held(k), ar.at[8 + k]).wait()

    nt = (((1,), (1,)), ((), ()))
    of_row = iota((8, 64), 1)
    fold = (of_row // 8 % 4 * 2 + of_row // 2 % 2 == iota((8, 64), 0)).astype(F32)

    @pl.loop(0, 5)
    def _(sp):
        lows, highs = fall[:, 0:4, sp], fall[:, 4:8, sp]
        low = lows.astype(F32).reshape(64, 640).astype(BF16)
        high = highs.astype(F32).reshape(64, 640).astype(BF16)
        for s2 in range(2):
            basis = leg[2 * sp + s2]
            sums = lax.dot_general(low, basis[:, :640], nt, preferred_element_type=F32)
            sums += lax.dot_general(high, basis[:, 640:], nt, preferred_element_type=F32)
            sums = sums * fac[2 * sp + s2]
            folded = jnp.dot(fold, sums, preferred_element_type=F32, precision=lax.Precision.HIGHEST)
            done = (spec_t[2 * sp + s2] + folded) * mul_t[2 * sp + s2]
            for f in range(4):
                spec_out[f, 2 * sp + s2] = done[2 * f : 2 * f + 2]

    for n in range(4):
        swap(n, 8 - step).wait_send()
    for copy in opening + [ahead, behind]:
        copy.wait_send()
    for k, have in hops.items():
        around(k, have).wait_send()
    for k in range(8):
        across(k).wait_send()
    rest = brcv.at[pl.ds(0, 63)]
    pltpu.make_async_copy(rest, rest, bs).wait()
    pltpu.make_async_copy(rest, rest, es).wait()

    @pl.loop(0, 16)
    def _(n):
        settle(*forcing_copy(n))
        settle(*grid_copy(n))

    settle(*rows_copy())


def body(spec, legendre, wave_pairs, row_waves, forcing, helm_coef):
    vmem, hbm = pl.BlockSpec(memory_space=pltpu.VMEM), pl.BlockSpec(memory_space=pl.ANY)
    dma = pltpu.SemaphoreType.DMA

    def v16(*shape):
        return pltpu.VMEM(shape, BF16)

    def v32(*shape):
        return pltpu.VMEM(shape, F32)

    def v_i(*shape):
        return pltpu.VMEM(shape, I32)

    grid_field, spec_new = pl.pallas_call(
        kernel,
        out_shape=(
            v32(4, 40, SEG),
            v32(4, 10, 2, 84),
        ),
        in_specs=[hbm] * 12,
        out_specs=(vmem, vmem),
        scratch_shapes=[
            v16(10, 84, M), v32(4, 40, SEG), v16(3104, 256), v16(512, 512), v16(80, SEG),
            v32(4, 10, 2, 84), v_i(5, 128), v_i(1, 40), v32(1, 4), v_i(2, 16, 512), v_i(2, 8, M), v_i(8, M),
            v32(16, 128), v32(10, 8, 84),
            v16(10, 64, 84), v32(10, 64, 84), v32(10, 8, 84), v32(4, 4, 16, SEG), v16(4, 4, 8, SEG), v16(4, 4, 2, SEG), v32(8, 128),
            v16(2, 4, 5, 8, M), v16(4, 5, 8, M), v16(4, 5, 8, M), v16(8, 5, 8, 640), v16(2, 5, 8, 640),
            v32(128, 640), v32(640, 128), v16(10, 128, 512), v16(512, M), v16(3, 640, 256), v16(768, 640),
            v16(640, M), v32(64, 4, 128), v32(64, 4, 128), v16(16, 8, SEG), v16(16, 2, SEG), v32(16, 16, SEG), v32(8, 128),
            v16(640, 240), v16(16, 8, SEG), v16(16, 2, SEG), v16(4, 4, 8, SEG), v16(4, 4, 2, SEG), v16(3, 640, 128), v32(64, 4, 128),
            v32(64, 4, 128), v16(2, 8, 5, 8, 640),
            dma((12,)), dma((2, 4)), dma((2, 16)), dma((2,)), dma((8,)), dma((8,)), dma, dma, dma, dma,
            dma((2, 16)), dma((2,)), dma((16,)), dma((16,)), dma, dma,
        ],
        compiler_params=pltpu.CompilerParams(
            collective_id=0, has_side_effects=True, vmem_limit_bytes=60 * 1024 * 1024
        ),
        name="step",
    )(
        legendre, forcing, *tables()[:3], jnp.transpose(spec, (0, 2, 1, 3)), wave_pairs.reshape(5, 128),
        row_waves.reshape(1, 40), helm_coef.reshape(1, 4), *tables()[3:],
    )
    return (grid_field, jnp.transpose(spec_new, (0, 2, 1, 3)))


def solution(mesh):
    return jax.shard_map(
        body,
        mesh=mesh,
        in_specs=(
            P(None, None, "lat", "lon"),
            P("lat", "lon", None),
            P(),
            P("lat"),
            P(None, "lat", "lon"),
            P(),
        ),
        out_specs=(P(None, "lat", "lon"), P(None, None, "lat", "lon")),
        check_vma=False,
    )
```
